32 devices in a mesh: dp: 4 (over y, core), expert: 8 (over z, x).
Axes of the slice: x: 2, y: 2, z: 4, core: 2. Of those that a mesh axis runs over, the one named last changes fastest.
Arguments:
- tokens: bfloat16 [1024, 7168], P('expert', 'dp'), may hold values from -6 to 6
- routes: int32 [1024, 8], P('expert'), may hold values from 0 to 31, all different within a row; in each aligned block of 128 rows (0 to 127, 128 to 255, ...) at most 64 rows name the same one
- route_weight: float32 [1024, 8], P('expert'), may hold values from 0.1 to 1
- gate_first: bfloat16 [32, 64, 112, 32], P('expert', 'dp'), may hold values from -0.5 to 0.5
- up_first: bfloat16 [32, 64, 112, 32], P('expert', 'dp'), may hold values from -0.5 to 0.5
- gate_second: bfloat16 [32, 32, 64, 64], P('expert', 'dp'), may hold values from -0.75 to 0.75
- up_second: bfloat16 [32, 32, 64, 64], P('expert', 'dp'), may hold values from -0.75 to 0.75
- down_first: bfloat16 [32, 32, 64, 64], P('expert', 'dp'), may hold values from -0.75 to 0.75
- down_second: bfloat16 [32, 64, 32, 112], P('expert', 'dp'), may hold values from -1 to 1
Outputs:
- moe_output: bfloat16 [1024, 7168], P('expert', 'dp')
- expert_load: float32 [32], P('expert')
The draws below stay inside these ranges and needn't reach their ends.
Inputs may be any that keep to these rules, and one draw needn't show every extreme that they name: `routes`: each row names 8 different experts. Within each device's aligned block of 128 rows no expert is named by more than 64 rows, and in some block an expert is named by exactly 64 rows.
All inputs are finite; a program needn't handle non-finite values.
Results may differ from the reference program's by a relative error of at most 0.0076.
Values may be sent and summed in bfloat16 or wider, within the bound.
A program may use at most 64 MiB of HBM per device.

```python
import math
import jax
import jax.numpy as jnp
import numpy as np
from jax import lax

D = 7168
TOP = 8
BLOCKS = 64
TOK_DEV = 128
EXPERTS = 32
TOKENS = 1024
CAP = 64
BW = 112
RANK = 32
N_EXPERT = 8


def block_scale(rng, shape, pieces, smallest, top_value):
    def one(axis_at, parts):
        heights = jax.random.uniform(jax.random.fold_in(jax.random.fold_in(rng, 6), axis_at), (parts,), jnp.float32, smallest / len(pieces), top_value / len(pieces))
        return jnp.repeat(jnp.exp(heights), shape[axis_at] // parts).reshape((-1,) + (1,) * (len(shape) - axis_at - 1))

    level = one(*pieces[0])
    for cut in pieces[1:]:
        level = level * one(*cut)
    return level


def deal_out(key, own, number, rows, number_of, top, bound, lean):
    ranking = jax.random.permutation(key, number_of)
    packed, ordinary = shares(number_of, rows * top, bound, lean, True), shares(number_of, rows * top, bound, lean, False)
    places = jnp.arange(number_of)

    def named(sizes, rotation):
        used = int((sizes > 0).sum())
        fixed = max(1, used // 4)
        moved = fixed + (places - fixed + rotation * (used - fixed)) % max(1, number_of - fixed)
        return jnp.zeros((number_of,), jnp.int32).at[ranking[jnp.where(places < fixed, places, moved)]].set(jnp.asarray(sizes, jnp.int32))

    sizes = jnp.where(number % 4 == 0, named(packed, number // 4), named(ordinary, number - number // 4 - 1))
    mixed = jax.random.permutation(jax.random.fold_in(own, 3), number_of)
    source_of, taker = mixed[0:number_of // 2 * 2:2], mixed[1:number_of // 2 * 2:2]
    slack = jnp.minimum(sizes[source_of] - 1, bound - sizes[taker]) // 2
    slack = jnp.where((source_of == ranking[0]) | (taker == ranking[0]) | (sizes[taker] == 0), 0, jnp.maximum(slack, 0))
    moved = jax.random.randint(jax.random.fold_in(own, 4), (number_of // 2,), 0, 1 << 20) % (slack + 1)
    sizes = sizes.at[source_of].add(-moved).at[taker].add(moved)
    items = jnp.searchsorted(jnp.cumsum(sizes), jnp.arange(rows * top), side="right").astype(jnp.int32)
    table = items.reshape(top, rows).T
    table = table[jax.random.permutation(jax.random.fold_in(own, 1), rows)]
    rotation = jax.random.randint(jax.random.fold_in(own, 2), (rows, 1), 0, top)
    return jnp.take_along_axis(table, (jnp.arange(top)[None, :] + rotation) % top, axis=1)


def shares(amount, total, limit, slope, full):
    loads = [(1 << 20) // math.isqrt(grade ** slope) + 1 for grade in range(1, amount + 1)]
    largest = limit if full else min(limit, max(-(-total // amount), total * loads[0] // sum(loads)))
    least = 1 if total - largest >= amount - 1 else 0
    given, surplus = [largest] + [least] * (amount - 1), total - largest - least * (amount - 1)
    while surplus > 0:
        free = [i for i in range(1, amount) if given[i] < largest] or [i for i in range(1, amount) if given[i] < limit]
        whole, left = sum([loads[i] for i in free]), surplus
        for i in free:
            more = min(limit - given[i], max(1, left * loads[i] // whole), surplus)
            given[i] = given[i] + more
            surplus = surplus - more
    return np.array(given)


def centred(own_key, extent, deviation, bound, cuts=(), kind=jnp.bfloat16):
    factor_of = block_scale(own_key, extent, cuts, -0.22, 0.18) if cuts else 1.0
    entries = jax.random.normal(own_key, extent, jnp.float32) * deviation * factor_of
    return jnp.minimum(jnp.maximum(entries, -bound), bound).astype(kind)


def setup_inputs(seed: int = 0) -> dict:
    key_list = jax.random.split(jax.random.key(seed), 10)
    tokens = centred(key_list[0], (TOKENS, D), 1.0, 6.0, ((0, 8), (1, 4)))
    routes_keys = jax.random.split(jax.random.fold_in(key_list[1], 1), TOKENS // TOK_DEV)
    routes_turns = jax.random.permutation(jax.random.fold_in(key_list[1], 3), TOKENS // TOK_DEV)
    routes = jax.vmap(lambda own, number: deal_out(jax.random.fold_in(key_list[1], 2), own, number, TOK_DEV, EXPERTS, TOP, CAP, 2))(routes_keys, routes_turns).reshape((TOKENS, TOP))
    route_weight = jnp.clip(jnp.exp(math.log(1.0) - 2.3025851 * jax.random.uniform(key_list[2], (TOKENS, TOP), jnp.float32) ** block_scale(key_list[2], (TOKENS, TOP), ((0, 8),), -0.2, 0.2)), 0.1, 1.0)
    gate_first = centred(key_list[3], (EXPERTS, BLOCKS, BW, RANK), BW ** -0.5, 0.5, ((0, 8), (1, 4)))
    up_first = centred(key_list[4], (EXPERTS, BLOCKS, BW, RANK), BW ** -0.5, 0.5, ((0, 8), (1, 4)))
    gate_second = centred(key_list[5], (EXPERTS, RANK, BLOCKS, BLOCKS), BLOCKS ** -0.5, 0.75, ((0, 8), (1, 4)))
    up_second = centred(key_list[6], (EXPERTS, RANK, BLOCKS, BLOCKS), BLOCKS ** -0.5, 0.75, ((0, 8), (1, 4)))
    down_first = centred(key_list[7], (EXPERTS, RANK, BLOCKS, BLOCKS), BLOCKS ** -0.5, 0.75, ((0, 8), (1, 4)))
    down_second = centred(key_list[8], (EXPERTS, BLOCKS, RANK, BW), RANK ** -0.5, 1.0, ((0, 8), (1, 4)))
    return dict(tokens=tokens, routes=routes, route_weight=route_weight, gate_first=gate_first, up_first=up_first, gate_second=gate_second, up_second=up_second, down_first=down_first, down_second=down_second)


def rounded(value):
    return lax.optimization_barrier(value.astype(jnp.bfloat16)).astype(jnp.float32)


def monarch_expert(picked_rows, expert_id, gate_first, up_first, gate_second, up_second, down_first, down_second):
    row_count = picked_rows.shape[0]
    shaped = picked_rows.reshape(row_count, BLOCKS, BW).astype(jnp.float32)
    gate_low = rounded(jnp.einsum("nbf,bfr->nbr", shaped, gate_first[expert_id].astype(jnp.float32)))
    up_low = rounded(jnp.einsum("nbf,bfr->nbr", shaped, up_first[expert_id].astype(jnp.float32)))
    gate_high = jnp.einsum("nbc,cbm->ncm", gate_low, gate_second[expert_id].astype(jnp.float32))
    up_high = jnp.einsum("nbc,cbm->ncm", up_low, up_second[expert_id].astype(jnp.float32))
    activated = rounded(jax.nn.silu(gate_high) * up_high)
    down_low = rounded(jnp.einsum("ncm,cmo->nco", activated, down_first[expert_id].astype(jnp.float32)))
    expert_out = jnp.einsum("ncb,bcf->nbf", down_low, down_second[expert_id].astype(jnp.float32))
    return expert_out.astype(jnp.bfloat16).reshape(row_count, D)


def reference(tokens, routes, route_weight, gate_first, up_first, gate_second, up_second, down_first, down_second):
    capacity_rows = N_EXPERT * CAP

    def one_expert(accumulated, expert_id):
        routed_here = routes == expert_id
        row_weight = jnp.sum(jnp.where(routed_here, route_weight, jnp.float32(0.0)), axis=1)
        chosen = jnp.any(routed_here, axis=1)
        picked_index = jnp.nonzero(chosen, size=capacity_rows, fill_value=TOKENS)[0].astype(jnp.int32)
        picked_rows = jnp.take(tokens, picked_index, axis=0, mode="fill", fill_value=0)
        expert_out = monarch_expert(picked_rows, expert_id, gate_first, up_first, gate_second, up_second, down_first, down_second)
        row_share = jnp.take(row_weight, picked_index, axis=0, mode="fill", fill_value=0)
        accumulated = accumulated.at[picked_index].add(expert_out.astype(jnp.float32) * row_share[:, None], mode="drop")
        return accumulated, jnp.sum(chosen.astype(jnp.int32))

    start = jnp.zeros((TOKENS, D), jnp.float32)
    accumulated, counts = lax.scan(one_expert, start, jnp.arange(EXPERTS, dtype=jnp.int32))
    moe_output = accumulated.astype(jnp.bfloat16)
    expert_load = counts.astype(jnp.float32) * EXPERTS / (TOKENS * TOP)
    return (moe_output, expert_load)
```

```python
import functools

import jax
import jax.numpy as jnp
from jax import lax
from jax.experimental import pallas as pl
from jax.experimental.pallas import tpu as pltpu
from jax.sharding import PartitionSpec as P

F32 = jnp.float32
BF16 = jnp.bfloat16
MESH = pl.DeviceIdType.MESH
LAGS = (3, 6)


def shards(
    tokens,
    routes,
    route_weight,
    gate_first,
    up_first,
    gate_second,
    up_second,
    down_first,
    down_second,
):
    tok_rows, width_here = tokens.shape
    top_k = routes.shape[1]
    groups = lax.axis_size("expert")
    dp_count = lax.axis_size("dp")
    per_dev, blocks_here, block_width, rank_size = gate_first.shape
    rank_here = gate_second.shape[1]
    block_count = gate_second.shape[2]
    experts = per_dev * groups
    capacity = 2 * tok_rows * top_k // experts
    flat_routes = routes.reshape(-1)
    pair_count = flat_routes.shape[0]
    one_hot = (flat_routes[:, None] == jnp.arange(experts, dtype=jnp.int32)[None, :]).astype(
        jnp.int32
    )
    earlier = jnp.cumsum(one_hot, axis=0) - one_hot
    position = jnp.sum(earlier * one_hot, axis=1)
    counts = jnp.sum(one_hot, axis=0)
    slot_index = flat_routes * capacity + position
    pair_token = jnp.arange(pair_count, dtype=jnp.int32) // top_k
    slot_token = jnp.full((experts * capacity,), tok_rows, jnp.int32).at[slot_index].set(pair_token)
    outgoing = jnp.take(tokens, slot_token, axis=0, mode="fill", fill_value=0).reshape(
        groups, per_dev, capacity, width_here
    )
    gate_wide = gate_second.reshape(per_dev, rank_here, dp_count, blocks_here, block_count)
    up_wide = up_second.reshape(per_dev, rank_here, dp_count, blocks_here, block_count)
    down_wide = down_second.reshape(per_dev, blocks_here, dp_count, rank_here, block_width)
    received = lax.all_to_all(outgoing, "expert", split_axis=0, concat_axis=0, tiled=True)
    sources = received.shape[0]
    local = received.shape[1]
    slots = received.shape[2]
    split_rows = received.reshape(sources, local, slots, blocks_here, block_width)
    gate_low = jnp.einsum(
        "aesbf,ebfr->rbeas", split_rows, gate_first, preferred_element_type=jnp.float32
    )
    up_low = jnp.einsum(
        "aesbf,ebfr->rbeas", split_rows, up_first, preferred_element_type=jnp.float32
    )
    layout = (dp_count, rank_here, blocks_here, local, sources, slots)
    gate_mixed = lax.all_to_all(
        gate_low.astype(jnp.bfloat16).reshape(layout), "dp", split_axis=0, concat_axis=0, tiled=True
    )
    up_mixed = lax.all_to_all(
        up_low.astype(jnp.bfloat16).reshape(layout), "dp", split_axis=0, concat_axis=0, tiled=True
    )
    gate_high = jnp.einsum(
        "qcjeas,ecqjm->ecmas", gate_mixed, gate_wide, preferred_element_type=jnp.float32
    )
    up_high = jnp.einsum(
        "qcjeas,ecqjm->ecmas", up_mixed, up_wide, preferred_element_type=jnp.float32
    )
    activated = (jax.nn.silu(gate_high) * up_high).astype(jnp.bfloat16)
    down_low = jnp.einsum(
        "ecmas,ecmn->ecnas", activated, down_first, preferred_element_type=jnp.float32
    )
    down_split = down_low.astype(jnp.bfloat16).reshape(
        local, rank_here, dp_count, blocks_here, sources, slots
    )
    down_mixed = lax.all_to_all(down_split, "dp", split_axis=2, concat_axis=2, tiled=True)
    expert_out = jnp.einsum(
        "ecqjas,ejqcf->aesjf", down_mixed, down_wide, preferred_element_type=jnp.float32
    )
    result = expert_out.astype(jnp.bfloat16).reshape(sources, local, slots, width_here)
    totals = lax.psum(counts, "expert")
    own_counts = lax.dynamic_slice_in_dim(
        totals, lax.axis_index("expert") * per_dev, per_dev
    ).astype(jnp.float32)
    returned = lax.all_to_all(result, "expert", split_axis=0, concat_axis=0, tiled=True).reshape(
        experts * capacity, width_here
    )
    picked = jnp.take(returned, slot_index, axis=0).astype(jnp.float32)
    weighted = picked * route_weight.reshape(-1)[:, None]
    moe_output = jnp.sum(weighted.reshape(tok_rows, top_k, width_here), axis=1).astype(jnp.bfloat16)
    expert_load = own_counts * experts / (tok_rows * groups * top_k)
    return (moe_output, expert_load)


def xor(a, b, count):
    total, bit = 0, 1
    while bit < count:
        total = total + bit * ((a // bit + b // bit) % 2)
        bit *= 2
    return total


def dot(a, b):
    return jnp.dot(a, b, preferred_element_type=F32)


def one_hot(hit):
    return jnp.where(hit, F32(1), F32(0)).astype(BF16)


def swap_groups(a, b, size):
    lane = lax.broadcasted_iota(jnp.int32, a.shape, len(a.shape) - 1)
    even = (lane // size) % 2 == 0
    axis = len(a.shape) - 1
    first = jnp.where(even, a, pltpu.roll(b, size, axis))
    second = jnp.where(even, pltpu.roll(a, 128 - size, axis), b)
    return first, second


def expert_kernel(
    sizes,
    tok, routes, shares_in, gf, uf, gs_in, us_in, df_in, ds,
    out, load,
    tok_all, routes_all, shares_all, gs, df, gf2, uf2, gs2, df2, ds2,
    w1, w2, w3, w4, place1, place3, rows,
    low_out, low_in, down_out, down_in,
    combine, made, summed, z_out, z_in, counts, counts_in,
    gather_s, gather_r, weight_s, weight_r, low_s, low_r, down_s, down_r,
    local_low, local_down, count_s, z_s, z_r,
):
    groups, dp, top_k, cap, rank_here, block_count = sizes
    per_dev, blocks, rank, width = gf.shape
    tok_rows, features = tok.shape
    experts = per_dev * groups
    half = blocks // 2
    half_width = half * width
    chunk = 2 * rank_here * half
    hidden = rank_here * block_count
    pairs = rank_here // 2
    quad = pairs * block_count
    nz = groups // 2
    steps = 2 * nz
    units = steps * per_dev
    ring = low_out.shape[0]
    lag_b, lag_c = LAGS
    d = lax.axis_index("dp")
    g = lax.axis_index("expert")
    z, x = g // 2, g % 2
    partner = (d, z * 2 + (1 - x))
    inner = (z >= 1) & (z < nz - 1)

    def at_dp(r):
        return (xor(d, r, dp), g)

    def at_z(k):
        return (d, xor(z, k, nz) * 2 + x)

    def remote(src, dst, send, recv, to):
        return pltpu.make_async_remote_copy(
            src_ref=src, dst_ref=dst, send_sem=send, recv_sem=recv,
            device_id=to, device_id_type=MESH,
        )

    barrier = pltpu.get_barrier_semaphore()
    peers = [at_dp(r) for r in range(1, dp)] + [partner] + [at_z(k) for k in range(1, nz)]
    for peer in peers:
        pl.semaphore_signal(barrier, inc=1, device_id=peer, device_id_type=MESH)
    pl.semaphore_wait(barrier, len(peers))

    own = ((routes, routes_all), (shares_in, shares_all), (tok, tok_all))

    def gather(link, source, to, slot):
        return [
            remote(
                src if source == 0 else dst.at[source], dst.at[slot],
                gather_s.at[n, link], gather_r.at[n, slot], at_z(to),
            )
            for n, (src, dst) in enumerate(own)
        ]

    sends = (gather(0, 0, 1, 1), gather(1, 0, 3, 3))
    relays = (gather(2, 1, 3, 2), gather(3, 3, 1, 2), gather(4, 2, 1, 3))

    def arrived(slot):
        for copy in gather(0, 0, 1, slot):
            copy.wait_recv()

    held = (gf, uf, gs, df, ds)
    swapped = (gf2, uf2, gs2, df2, ds2)

    def swap(n):
        return remote(held[n], swapped[n], weight_s.at[n], weight_r.at[n], partner)

    for copy in sends[0]:
        copy.start()

    @pl.when(inner)
    def _():
        for copy in sends[1]:
            copy.start()

    swap(0).start()
    swap(1).start()
    tok_all[0] = tok[...]
    routes_all[0] = routes[...]
    shares_all[0] = shares_in[...]
    counts[...] = jnp.zeros_like(counts)

    row1 = lax.broadcasted_iota(jnp.int32, (2 * rank, dp * chunk), 0)
    col1 = lax.broadcasted_iota(jnp.int32, (2 * rank, dp * chunk), 1)
    side1, rest1 = row1 // rank, row1 % rank
    base1 = (rest1 // rank_here) * chunk + side1 * (chunk // 2) + (rest1 % rank_here) * half
    for j in range(half):
        place1[j] = one_hot(col1 == base1 + j)

    def spread_first(e, turn, gate, up):
        for b in range(blocks):
            both = jnp.concatenate([gate[e, b], up[e, b]], axis=0)
            w1[turn, e, b] = lax.dot_general(
                both, place1[b % half], (((0,), (0,)), ((), ())), preferred_element_type=F32
            ).astype(BF16)

    def spread_middle(e, turn, second, third):
        lane = lax.broadcasted_iota(jnp.int32, (block_count, 128), 1)
        low_half = lane < block_count
        nothing = jnp.zeros((block_count // half, half, 128), F32)
        for part in range(rank_here // pairs):
            tiles = ([], [])
            for c in range(pairs):
                value = second[e, part * pairs + c].astype(F32)
                turned = pltpu.roll(value, block_count, 1)
                for side in range(2):
                    if c % 2 == 0:
                        kept = jnp.where(low_half, value if side == 0 else turned, F32(0))
                    else:
                        kept = jnp.where(low_half, F32(0), turned if side == 0 else value)
                    kept = kept.reshape(block_count // half, half, 128)
                    spots = [nothing] * (quad // 128)
                    spots[c // 2] = kept
                    tiles[side].append(jnp.concatenate(spots, axis=2))
            for side in range(2):
                tile = jnp.stack(tiles[side], axis=1).reshape(quad, quad)
                w2[turn, e, side * (rank_here // pairs) + part] = tile.astype(BF16)
        for c in range(rank_here):
            value = dot(third[e, c % pairs], place3[c])
            w3[turn, e, c * block_count : (c + 1) * block_count] = value.astype(BF16)

    def spread_last(e, turn, fourth):
        lane = lax.broadcasted_iota(jnp.int32, (rank, 128), 1)
        nothing = jnp.zeros((dp, rank_here, 128), F32)
        for h in range(2):
            stripes = []
            for n in range(half):
                value = fourth[e, h * half + n].astype(F32)
                value = jnp.concatenate(
                    [value, jnp.zeros((rank, 128 - width), F32)], axis=1
                )
                spot, shift = (n * width) // 128, (n * width) % 128
                spots = [nothing] * (half_width // 128)
                if shift == 0:
                    spots[spot] = value.reshape(dp, rank_here, 128)
                else:
                    turned = pltpu.roll(value, shift, 1)
                    spots[spot] = jnp.where(lane >= shift, turned, F32(0)).reshape(
                        dp, rank_here, 128
                    )
                    if shift + width > 128:
                        spots[spot + 1] = jnp.where(lane < shift, turned, F32(0)).reshape(
                            dp, rank_here, 128
                        )
                stripes.append(jnp.concatenate(spots, axis=2))
            tile = jnp.stack(stripes, axis=1).reshape(dp * chunk // 2, half_width)
            w4[turn, e, h] = tile.astype(BF16)

    def place_of(i):
        turn = i // nz
        return turn, (i % nz) * (1 - turn) + (nz - 1 - i % nz) * turn

    def low_copy(u, r):
        return remote(
            low_out.at[u % ring, xor(d, r, dp)], low_in.at[u, d],
            low_s.at[u % ring, r], low_r.at[u, r], at_dp(r),
        )

    def down_copy(u, r):
        return remote(
            down_out.at[u % ring, xor(d, r, dp)], down_in.at[u, d],
            down_s.at[u % ring, r], down_r.at[u, r], at_dp(r),
        )

    def low_local(u):
        return pltpu.make_async_copy(
            low_out.at[u % ring, d], low_in.at[u, d], local_low.at[u % ring]
        )

    def down_local(u):
        return pltpu.make_async_copy(
            down_out.at[u % ring, d], down_in.at[u, d], local_down.at[u % ring]
        )

    crossing = list(range(dp - 1, 0, -1))

    def pick_rows(i):
        turn, k = place_of(i)

        @pl.when(i == 1)
        def _():
            arrived(1)

            @pl.when(inner)
            def _():
                for copy in relays[0]:
                    copy.start()
                arrived(3)
                for copy in relays[1]:
                    copy.start()

        @pl.when(i == 2)
        def _():
            arrived(2)

            @pl.when(inner)
            def _():
                for copy in relays[2]:
                    copy.start()

        @pl.when((i == 3) & jnp.logical_not(inner))
        def _():
            arrived(3)

        base = (z * 2 + (x + turn) % 2) * per_dev
        named_rows, weights = routes_all[k], shares_all[k]
        line = lax.broadcasted_iota(jnp.int32, (8, tok_rows), 0)
        hits = jnp.zeros((8, tok_rows), F32)
        shares = []
        for e in range(per_dev):
            named = named_rows == base + e
            hit = jnp.max(jnp.where(named, F32(1), F32(0)), axis=0, keepdims=True)
            hits = hits + jnp.where(line == e, hit, F32(0))
            shares.append(jnp.sum(jnp.where(named, weights, F32(0)), axis=0, keepdims=True))
        counts[turn] += hits
        before = lax.broadcasted_iota(jnp.int32, (tok_rows, tok_rows), 0)
        after = lax.broadcasted_iota(jnp.int32, (tok_rows, tok_rows), 1)
        position = dot(hits.astype(BF16), one_hot(before < after))
        position = jnp.where(hits > 0, position, F32(-1)).astype(jnp.int32)
        slot_row = lax.broadcasted_iota(jnp.int32, (cap, tok_rows), 0)
        pick, mix = [], []
        for e in range(per_dev):
            chosen = slot_row == position[e : e + 1]
            pick.append(jnp.where(chosen, F32(1), F32(0)))
            mix.append(jnp.where(chosen, shares[e], F32(0)))
        pick = jnp.concatenate(pick, axis=0).astype(BF16)
        combine[i] = jnp.concatenate(mix, axis=0).T.astype(BF16)
        rows[...] = dot(pick, tok_all[k]).astype(BF16).reshape(per_dev, cap, features)

    def stage_a(u):
        i, e = u // per_dev, u % per_dev
        turn = i // nz

        @pl.when(u >= ring)
        def _():
            for r in crossing:
                low_copy(u - ring, r).wait_send()

        @pl.when(e == 0)
        def _():
            pick_rows(i)

        for h in range(2):
            weight = w1[turn, e, h * half : (h + 1) * half].reshape(half_width, dp * chunk)
            low = dot(rows[e, :, h * half_width : (h + 1) * half_width], weight).astype(BF16)
            for q in range(dp):
                low_out[u % ring, q, h] = low[:, q * chunk : (q + 1) * chunk]
        for r in crossing:
            low_copy(u, r).start()
        low_local(u).start()

    def stage_b(u):
        i, e = u // per_dev, u % per_dev
        turn = i // nz
        low_local(u).wait()
        for r in crossing:
            low_copy(u, r).wait_recv()

        @pl.when(u >= ring)
        def _():
            for r in crossing:
                down_copy(u - ring, r).wait_send()

        groups_of = []
        for lead in range(0, dp, 2):
            a, b, c_, d_ = [low_in[u, p, h] for p in (lead, lead + 1) for h in range(2)]
            a, c_ = swap_groups(a, c_, 64)
            b, d_ = swap_groups(b, d_, 64)
            a, b = swap_groups(a, b, 32)
            c_, d_ = swap_groups(c_, d_, 32)
            groups_of.append((a, b, c_, d_))
        high = [
            dot(jnp.concatenate([group[n] for group in groups_of], axis=1), w2[turn, e, n])
            for n in range(4)
        ]
        gate = jnp.concatenate(high[:2], axis=1)
        up = jnp.concatenate(high[2:], axis=1)
        activated = (gate / (1 + jnp.exp(-gate)) * up).astype(BF16)
        down = dot(activated, w3[turn, e]).astype(BF16)
        for p in range(dp):
            down_out[u % ring, p] = down[:, p * chunk : (p + 1) * chunk]
        for r in crossing:
            down_copy(u, r).start()
        down_local(u).start()

    def z_part(n, slot, to, h):
        return remote(z_out.at[n, h], z_in.at[slot, h], z_s.at[n, h], z_r.at[slot, h], at_z(to))

    def z_send(n, slot, to, h, value):
        z_out[n, h] = value.astype(BF16)
        z_part(n, slot, to, h).start()

    def z_wait(slot, h):
        z_part(0, slot, 1, h).wait_recv()

    def pass_far(h):
        z_wait(3, h)
        z_send(1, 4, 3, h, summed[2, h] + z_in[3, h].astype(F32))

    def pass_near(h):
        z_wait(4, h)
        z_send(0, 0, 1, h, summed[1, h] + z_in[4, h].astype(F32))

    def pass_across(h):
        z_wait(2, h)
        z_send(2, 5, 3, h, summed[3, h] + z_in[2, h].astype(F32))

    def stage_c(u):
        i, e = u // per_dev, u % per_dev
        turn, k = place_of(i)
        down_local(u).wait()
        for r in crossing:
            down_copy(u, r).wait_recv()
        pieces = [down_in[u, q] for q in range(dp)]
        low_a, high_a = swap_groups(pieces[0], pieces[1], 64)
        low_b, high_b = swap_groups(pieces[2], pieces[3], 64)
        for h, value in enumerate(((low_a, low_b), (high_a, high_b))):
            result = dot(jnp.concatenate(value, axis=1), w4[turn, e, h])
            made[h, e] = result.astype(BF16)

        @pl.when(e == per_dev - 1)
        def _():
            for h in range(2):
                part = dot(combine[i], made[h].reshape(per_dev * cap, half_width))

                @pl.when(turn == 0)
                def _():
                    summed[k, h] = part

                @pl.when((turn == 1) & ((k == 0) | inner))
                def _():
                    summed[k, h] += part

                for n in range(1, nz):

                    @pl.when((turn == 1) & (k == n) & jnp.logical_not(inner))
                    def _():
                        z_send(n - 1, n, 1, h, summed[n, h] + part)

    count_copy = remote(counts.at[1], counts_in, count_s.at[0], count_s.at[1], partner)

    for e in range(per_dev):
        for c in range(rank_here):
            gs[e, c] = jnp.concatenate([gs_in[e, c], us_in[e, c]], axis=1)
        for c in range(pairs):
            df[e, c] = jnp.concatenate([df_in[e, c], df_in[e, c + pairs]], axis=1)
    for n in range(2, 5):
        swap(n).start()
    row3 = lax.broadcasted_iota(jnp.int32, (2 * block_count, hidden), 0)
    col3 = lax.broadcasted_iota(jnp.int32, (2 * block_count, hidden), 1)
    for c in range(rank_here):
        offset = (c // pairs) * block_count
        hit = (row3 >= offset) & (row3 < offset + block_count)
        place3[c] = one_hot(hit & (col3 == (row3 - offset) * rank_here + c))

    far_steps = nz * per_dev
    first_at, middle_at = far_steps - per_dev - 1, far_steps + 1
    last_at = far_steps + lag_c

    @pl.loop(0, units + lag_c)
    def _(t):
        @pl.when(t < per_dev)
        def _():
            spread_first(t, 0, gf, uf)

        @pl.when((t >= first_at) & (t < first_at + per_dev))
        def _():
            @pl.when(t == first_at)
            def _():
                swap(0).wait_recv()
                swap(1).wait_recv()

            spread_first(t - first_at, 1, gf2, uf2)

        @pl.when(t < units)
        def _():
            stage_a(t)

        @pl.when((t >= lag_b) & (t < lag_b + per_dev))
        def _():
            spread_middle(t - lag_b, 0, gs, df)

        @pl.when((t >= middle_at) & (t < middle_at + per_dev))
        def _():
            @pl.when(t == middle_at)
            def _():
                swap(2).wait_recv()
                swap(3).wait_recv()

            spread_middle(t - middle_at, 1, gs2, df2)

        @pl.when((t >= lag_b) & (t < units + lag_b))
        def _():
            stage_b(t - lag_b)

        @pl.when((t >= lag_c) & (t < lag_c + per_dev))
        def _():
            spread_last(t - lag_c, 0, ds)

        @pl.when((t >= last_at) & (t < last_at + per_dev))
        def _():
            @pl.when(t == last_at)
            def _():
                swap(4).wait_recv()

            spread_last(t - last_at, 1, ds2)

        @pl.when(t >= lag_c)
        def _():
            stage_c(t - lag_c)

        @pl.when(t == units)
        def _():
            count_copy.start()

        done_far = (steps - 2) * per_dev + lag_c - 1
        for h in range(2):

            @pl.when(inner & (t == done_far + h))
            def _():
                pass_far(h)

        @pl.when(inner & (t == done_far + per_dev))
        def _():
            pass_across(0)

        @pl.when(inner & (t == done_far + per_dev + 1))
        def _():
            pass_near(0)

    @pl.when(inner)
    def _():
        pass_near(1)
        pass_across(1)

    count_copy.wait()
    ones = jnp.ones((8, tok_rows), BF16)
    held_rows = lax.dot_general(
        ones, (counts[0] + counts_in[...]).astype(BF16),
        (((1,), (1,)), ((), ())), preferred_element_type=F32,
    )
    load[...] = held_rows[:1, :per_dev] * experts / (tok_rows * groups * top_k)

    for h in range(2):
        span = slice(h * half_width, (h + 1) * half_width)

        @pl.when(inner)
        def _():
            z_wait(1, h)
            z_wait(5, h)
            both = z_in[1, h].astype(F32) + z_in[5, h].astype(F32)
            out[:, span] = (summed[0, h] + both).astype(BF16)

        @pl.when(jnp.logical_not(inner))
        def _():
            z_wait(0, h)
            out[:, span] = (summed[0, h] + z_in[0, h].astype(F32)).astype(BF16)

    for copy in sends[0]:
        copy.wait_send()

    @pl.when(inner)
    def _():
        for copies in (sends[1],) + relays:
            for copy in copies:
                copy.wait_send()

    for n in range(3):
        for h in range(2):
            z_part(n, 0, 1, h).wait_send()
    for n in range(len(held)):
        swap(n).wait_send()

    @pl.loop(units - ring, units)
    def _(u):
        for r in crossing:
            low_copy(u, r).wait_send()
            down_copy(u, r).wait_send()


def fused(
    tokens, routes, route_weight,
    gate_first, up_first, gate_second, up_second, down_first, down_second,
):
    tok_rows, features = tokens.shape
    top_k = routes.shape[1]
    groups = lax.axis_size("expert")
    dp = lax.axis_size("dp")
    per_dev, blocks, width, rank = gate_first.shape
    rank_here, block_count = gate_second.shape[1:3]
    experts = per_dev * groups
    cap = 2 * tok_rows * top_k // experts
    nz = groups // 2
    steps = 2 * nz
    units = steps * per_dev
    ring = 8
    half = blocks // 2
    chunk = 2 * rank_here * half
    hidden = rank_here * block_count
    slots = per_dev * cap
    pairs = rank_here // 2
    quad = pairs * block_count
    half_width = half * width
    first = (per_dev, blocks, rank, width)
    joined = (per_dev, rank_here, block_count, 2 * block_count)
    paired = (per_dev, pairs, block_count, 2 * block_count)
    last = down_second.shape
    vmem = pl.BlockSpec(memory_space=pltpu.VMEM)
    dma = pltpu.SemaphoreType.DMA
    out, load = pl.pallas_call(
        functools.partial(expert_kernel, (groups, dp, top_k, cap, rank_here, block_count)),
        out_shape=(
            jax.ShapeDtypeStruct((tok_rows, features), BF16),
            jax.ShapeDtypeStruct((1, per_dev), F32),
        ),
        in_specs=[vmem] * 9,
        out_specs=(vmem, vmem),
        scratch_shapes=[
            pltpu.VMEM((nz, tok_rows, features), BF16),
            pltpu.VMEM((nz, top_k, tok_rows), jnp.int32),
            pltpu.VMEM((nz, top_k, tok_rows), F32),
            *[pltpu.VMEM(s, BF16) for s in (joined, paired)],
            *[pltpu.VMEM(s, BF16) for s in (first, first, joined, paired, last)],
            pltpu.VMEM((2, per_dev, blocks, width, dp * chunk), BF16),
            pltpu.VMEM((2, per_dev, 4, quad, quad), BF16),
            pltpu.VMEM((2, per_dev, hidden, hidden), BF16),
            pltpu.VMEM((2, per_dev, 2, dp * chunk // 2, half_width), BF16),
            pltpu.VMEM((half, 2 * rank, dp * chunk), BF16),
            pltpu.VMEM((rank_here, 2 * block_count, hidden), BF16),
            pltpu.VMEM((per_dev, cap, features), BF16),
            pltpu.VMEM((ring, dp, 2, cap, chunk), BF16),
            pltpu.VMEM((units, dp, 2, cap, chunk), BF16),
            pltpu.VMEM((ring, dp, cap, chunk), BF16),
            pltpu.VMEM((units, dp, cap, chunk), BF16),
            pltpu.VMEM((steps, tok_rows, slots), BF16),
            pltpu.VMEM((2, per_dev, cap, half_width), BF16),
            pltpu.VMEM((nz, 2, tok_rows, half_width), F32),
            pltpu.VMEM((3, 2, tok_rows, half_width), BF16),
            pltpu.VMEM((6, 2, tok_rows, half_width), BF16),
            pltpu.VMEM((2, 8, tok_rows), F32),
            pltpu.VMEM((8, tok_rows), F32),
            dma((3, 5)), dma((3, nz)), dma((5,)), dma((5,)),
            dma((ring, dp)), dma((units, dp)), dma((ring, dp)), dma((units, dp)),
            dma((ring,)), dma((ring,)), dma((2,)), dma((3, 2)), dma((6, 2)),
        ],
        compiler_params=pltpu.CompilerParams(
            collective_id=0, has_side_effects=True, vmem_limit_bytes=67043328
        ),
    )(
        tokens, routes.T, route_weight.T, gate_first.swapaxes(2, 3), up_first.swapaxes(2, 3),
        gate_second, up_second, down_first, down_second,
    )
    return (out, load.reshape(per_dev))


def chosen_plan(tokens, routes, route_weight, *weights):
    groups = lax.axis_size("expert")
    dp = lax.axis_size("dp")
    blocks, width = weights[0].shape[1:3]
    rank_here, block_count = weights[2].shape[1:3]
    tiled = (
        tokens.shape[0] % 128 == 0
        and 2 * rank_here * (blocks // 2) == 128
        and rank_here == 8
        and weights[0].shape[0] <= 8
        and blocks // 2 == 8
        and block_count == 2 * dp * 8
        and (blocks // 2 * width) % 128 == 0
    )
    powers = groups & (groups - 1) == 0 and dp & (dp - 1) == 0
    if groups <= 2 * routes.shape[1] and groups == 8 and dp == 4 and powers and tiled:
        return fused(tokens, routes, route_weight, *weights)
    return shards(tokens, routes, route_weight, *weights)


def solution(mesh):
    return jax.shard_map(
        chosen_plan,
        mesh=mesh,
        in_specs=(
            P("expert", "dp"),
            P("expert", None),
            P("expert", None),
            P("expert", "dp", None, None),
            P("expert", "dp", None, None),
            P("expert", "dp", None, None),
            P("expert", "dp", None, None),
            P("expert", "dp", None, None),
            P("expert", "dp", None, None),
        ),
        out_specs=(P("expert", "dp"), P("expert")),
        check_vma=False,
    )
```

```python
import functools

import jax
import jax.numpy as jnp
from jax import lax
from jax.experimental import pallas as pl
from jax.experimental.pallas import tpu as pltpu
from jax.sharding import PartitionSpec as P

F32 = jnp.float32
BF16 = jnp.bfloat16
MESH = pl.DeviceIdType.MESH
LAGS = (2, 4)


def shards(
    tokens,
    routes,
    route_weight,
    gate_first,
    up_first,
    gate_second,
    up_second,
    down_first,
    down_second,
):
    tok_rows, width_here = tokens.shape
    top_k = routes.shape[1]
    groups = lax.axis_size("expert")
    dp_count = lax.axis_size("dp")
    per_dev, blocks_here, block_width, rank_size = gate_first.shape
    rank_here = gate_second.shape[1]
    block_count = gate_second.shape[2]
    experts = per_dev * groups
    capacity = 2 * tok_rows * top_k // experts
    flat_routes = routes.reshape(-1)
    pair_count = flat_routes.shape[0]
    one_hot = (flat_routes[:, None] == jnp.arange(experts, dtype=jnp.int32)[None, :]).astype(
        jnp.int32
    )
    earlier = jnp.cumsum(one_hot, axis=0) - one_hot
    position = jnp.sum(earlier * one_hot, axis=1)
    counts = jnp.sum(one_hot, axis=0)
    slot_index = flat_routes * capacity + position
    pair_token = jnp.arange(pair_count, dtype=jnp.int32) // top_k
    slot_token = jnp.full((experts * capacity,), tok_rows, jnp.int32).at[slot_index].set(pair_token)
    outgoing = jnp.take(tokens, slot_token, axis=0, mode="fill", fill_value=0).reshape(
        groups, per_dev, capacity, width_here
    )
    gate_wide = gate_second.reshape(per_dev, rank_here, dp_count, blocks_here, block_count)
    up_wide = up_second.reshape(per_dev, rank_here, dp_count, blocks_here, block_count)
    down_wide = down_second.reshape(per_dev, blocks_here, dp_count, rank_here, block_width)
    received = lax.all_to_all(outgoing, "expert", split_axis=0, concat_axis=0, tiled=True)
    sources = received.shape[0]
    local = received.shape[1]
    slots = received.shape[2]
    split_rows = received.reshape(sources, local, slots, blocks_here, block_width)
    gate_low = jnp.einsum(
        "aesbf,ebfr->rbeas", split_rows, gate_first, preferred_element_type=jnp.float32
    )
    up_low = jnp.einsum(
        "aesbf,ebfr->rbeas", split_rows, up_first, preferred_element_type=jnp.float32
    )
    layout = (dp_count, rank_here, blocks_here, local, sources, slots)
    gate_mixed = lax.all_to_all(
        gate_low.astype(jnp.bfloat16).reshape(layout), "dp", split_axis=0, concat_axis=0, tiled=True
    )
    up_mixed = lax.all_to_all(
        up_low.astype(jnp.bfloat16).reshape(layout), "dp", split_axis=0, concat_axis=0, tiled=True
    )
    gate_high = jnp.einsum(
        "qcjeas,ecqjm->ecmas", gate_mixed, gate_wide, preferred_element_type=jnp.float32
    )
    up_high = jnp.einsum(
        "qcjeas,ecqjm->ecmas", up_mixed, up_wide, preferred_element_type=jnp.float32
    )
    activated = (jax.nn.silu(gate_high) * up_high).astype(jnp.bfloat16)
    down_low = jnp.einsum(
        "ecmas,ecmn->ecnas", activated, down_first, preferred_element_type=jnp.float32
    )
    down_split = down_low.astype(jnp.bfloat16).reshape(
        local, rank_here, dp_count, blocks_here, sources, slots
    )
    down_mixed = lax.all_to_all(down_split, "dp", split_axis=2, concat_axis=2, tiled=True)
    expert_out = jnp.einsum(
        "ecqjas,ejqcf->aesjf", down_mixed, down_wide, preferred_element_type=jnp.float32
    )
    result = expert_out.astype(jnp.bfloat16).reshape(sources, local, slots, width_here)
    totals = lax.psum(counts, "expert")
    own_counts = lax.dynamic_slice_in_dim(
        totals, lax.axis_index("expert") * per_dev, per_dev
    ).astype(jnp.float32)
    returned = lax.all_to_all(result, "expert", split_axis=0, concat_axis=0, tiled=True).reshape(
        experts * capacity, width_here
    )
    picked = jnp.take(returned, slot_index, axis=0).astype(jnp.float32)
    weighted = picked * route_weight.reshape(-1)[:, None]
    moe_output = jnp.sum(weighted.reshape(tok_rows, top_k, width_here), axis=1).astype(jnp.bfloat16)
    expert_load = own_counts * experts / (tok_rows * groups * top_k)
    return (moe_output, expert_load)


def xor(a, b, count):
    total, bit = 0, 1
    while bit < count:
        total = total + bit * ((a // bit + b // bit) % 2)
        bit *= 2
    return total


def dot(a, b):
    return jnp.dot(a, b, preferred_element_type=F32)


def one_hot(hit):
    return jnp.where(hit, F32(1), F32(0)).astype(BF16)


def swap_groups(a, b, size):
    lane = lax.broadcasted_iota(jnp.int32, a.shape, len(a.shape) - 1)
    even = (lane // size) % 2 == 0
    axis = len(a.shape) - 1
    first = jnp.where(even, a, pltpu.roll(b, size, axis))
    second = jnp.where(even, pltpu.roll(a, 128 - size, axis), b)
    return first, second


def expert_kernel(
    sizes,
    tok, routes, shares_in, gf_arg, uf_arg, gs_arg, us_arg, df_arg, ds_arg,
    out, load,
    tok_all, routes_all, shares_all, gf, uf, gs_in, us_in, df_in, ds,
    gs, df, gf2, uf2, gs2, df2, ds2,
    w1, w2, w3, w4, place1, place3, rows,
    low_out, low_in, down_out, down_in,
    combine, made, summed, z_out, z_in, counts, counts_in,
    gather_s, gather_r, weight_s, weight_r, low_s, low_r, down_s, down_r,
    local_low, local_down, load_s, count_s, z_s, z_r,
):
    groups, dp, top_k, cap, rank_here, block_count = sizes
    per_dev, blocks, rank, width = gf.shape
    tok_rows, features = tok.shape
    experts = per_dev * groups
    half = blocks // 2
    half_width = half * width
    chunk = 2 * rank_here * half
    hidden = rank_here * block_count
    pairs = rank_here // 2
    quad = pairs * block_count
    nz = groups // 2
    steps = 2 * nz
    units = steps * per_dev
    ring = low_out.shape[0]
    lag_b, lag_c = LAGS
    d = lax.axis_index("dp")
    g = lax.axis_index("expert")
    z, x = g // 2, g % 2
    partner = (d, z * 2 + (1 - x))
    inner = (z >= 1) & (z < nz - 1)

    def at_dp(r):
        return (xor(d, r, dp), g)

    def at_z(k):
        return (d, xor(z, k, nz) * 2 + x)

    def remote(src, dst, send, recv, to):
        return pltpu.make_async_remote_copy(
            src_ref=src, dst_ref=dst, send_sem=send, recv_sem=recv,
            device_id=to, device_id_type=MESH,
        )

    barrier = pltpu.get_barrier_semaphore()
    peers = [at_dp(r) for r in range(1, dp)] + [partner, at_z(1)]

    def greet(peer):
        pl.semaphore_signal(barrier, inc=1, device_id=peer, device_id_type=MESH)

    for peer in peers:
        greet(peer)

    @pl.when(inner)
    def _():
        greet(at_z(3))

    inputs = (
        (gf_arg, gf), (uf_arg, uf), (routes, routes_all.at[0]), (shares_in, shares_all.at[0]),
        (tok, tok_all.at[0]), (gs_arg, gs_in), (us_arg, us_in), (df_arg, df_in), (ds_arg, ds),
    )
    loads = [
        pltpu.make_async_copy(src, dst, load_s.at[n]) for n, (src, dst) in enumerate(inputs)
    ]
    for copy in loads:
        copy.start()

    part_rows = tok_rows // 2

    def gather(link, source, to, slot, h):
        rows_of = pl.ds(h * part_rows, part_rows)
        pairs_of = [(tok_all.at[source, rows_of], tok_all.at[slot, rows_of])]
        if h == 0:
            pairs_of += [(ref.at[source], ref.at[slot]) for ref in (routes_all, shares_all)]
        return [
            remote(src, dst, gather_s.at[n + 3 * h, link], gather_r.at[n + 3 * h, slot], at_z(to))
            for n, (src, dst) in enumerate(pairs_of)
        ]

    def begin(copies):
        for copy in copies:
            copy.start()

    sends = ((0, 0, 1, 1), (1, 0, 3, 3))
    relays = ((2, 1, 3, 2), (3, 3, 1, 2), (4, 2, 1, 3))

    def arrived(slot, h):
        for copy in gather(0, 0, 1, slot, h):
            copy.wait_recv()

    held = (gf, uf, gs, df, ds)
    swapped = (gf2, uf2, gs2, df2, ds2)

    def swap(n):
        return remote(held[n], swapped[n], weight_s.at[n], weight_r.at[n], partner)

    counts[...] = jnp.zeros_like(counts)
    def make_places():
        row1 = lax.broadcasted_iota(jnp.int32, (2 * rank, dp * chunk), 0)
        col1 = lax.broadcasted_iota(jnp.int32, (2 * rank, dp * chunk), 1)
        side1, rest1 = row1 // rank, row1 % rank
        base1 = (rest1 // rank_here) * chunk + side1 * (chunk // 2) + (rest1 % rank_here) * half
        for j in range(half):
            place1[j] = one_hot(col1 == base1 + j)

    def spread_first(e, turn, gate, up):
        for b in range(blocks):
            both = jnp.concatenate([gate[e, b], up[e, b]], axis=0)
            w1[turn, e, b] = lax.dot_general(
                both, place1[b % half], (((0,), (0,)), ((), ())), preferred_element_type=F32
            ).astype(BF16)

    def spread_middle(e, turn, second, third):
        lane = lax.broadcasted_iota(jnp.int32, (block_count, 128), 1)
        low_half = lane < block_count
        nothing = jnp.zeros((block_count // half, half, 128), F32)
        for part in range(rank_here // pairs):
            tiles = ([], [])
            for c in range(pairs):
                value = second[e, part * pairs + c].astype(F32)
                turned = pltpu.roll(value, block_count, 1)
                for side in range(2):
                    if c % 2 == 0:
                        kept = jnp.where(low_half, value if side == 0 else turned, F32(0))
                    else:
                        kept = jnp.where(low_half, F32(0), turned if side == 0 else value)
                    kept = kept.reshape(block_count // half, half, 128)
                    spots = [nothing] * (quad // 128)
                    spots[c // 2] = kept
                    tiles[side].append(jnp.concatenate(spots, axis=2))
            for side in range(2):
                tile = jnp.stack(tiles[side], axis=1).reshape(quad, quad)
                w2[turn, e, side * (rank_here // pairs) + part] = tile.astype(BF16)
        for c in range(rank_here):
            value = dot(third[e, c % pairs], place3[c])
            w3[turn, e, c * block_count : (c + 1) * block_count] = value.astype(BF16)

    def spread_last(e, turn, fourth):
        lane = lax.broadcasted_iota(jnp.int32, (rank, 128), 1)
        nothing = jnp.zeros((dp, rank_here, 128), F32)
        for h in range(2):
            stripes = []
            for n in range(half):
                value = fourth[e, h * half + n].astype(F32)
                value = jnp.concatenate(
                    [value, jnp.zeros((rank, 128 - width), F32)], axis=1
                )
                spot, shift = (n * width) // 128, (n * width) % 128
                spots = [nothing] * (half_width // 128)
                if shift == 0:
                    spots[spot] = value.reshape(dp, rank_here, 128)
                else:
                    turned = pltpu.roll(value, shift, 1)
                    spots[spot] = jnp.where(lane >= shift, turned, F32(0)).reshape(
                        dp, rank_here, 128
                    )
                    if shift + width > 128:
                        spots[spot + 1] = jnp.where(lane < shift, turned, F32(0)).reshape(
                            dp, rank_here, 128
                        )
                stripes.append(jnp.concatenate(spots, axis=2))
            tile = jnp.stack(stripes, axis=1).reshape(dp * chunk // 2, half_width)
            w4[turn, e, h] = tile.astype(BF16)

    def place_of(i):
        turn = i // nz
        return turn, (i % nz) * (1 - turn) + (nz - 1 - i % nz) * turn

    def low_copy(u, r):
        return remote(
            low_out.at[u % ring, xor(d, r, dp)], low_in.at[u, d],
            low_s.at[u % ring, r], low_r.at[u, r], at_dp(r),
        )

    def down_copy(u, r):
        return remote(
            down_out.at[u % ring, xor(d, r, dp)], down_in.at[u, d],
            down_s.at[u % ring, r], down_r.at[u, r], at_dp(r),
        )

    def low_local(u):
        return pltpu.make_async_copy(
            low_out.at[u % ring, d], low_in.at[u, d], local_low.at[u % ring]
        )

    def down_local(u):
        return pltpu.make_async_copy(
            down_out.at[u % ring, d], down_in.at[u, d], local_down.at[u % ring]
        )

    crossing = list(range(dp - 1, 0, -1))

    def pass_tokens(h):
        arrived(1, h)

        @pl.when(inner)
        def _():
            begin(gather(*relays[0], h))
            arrived(3, h)
            begin(gather(*relays[1], h))

    def pass_last(h):
        arrived(2, h)

        @pl.when(inner)
        def _():
            begin(gather(*relays[2], h))

    def meet(i):
        @pl.when(i == 1)
        def _():
            pass_tokens(1)

        @pl.when(i == 2)
        def _():
            pass_last(1)

        @pl.when((i == 3) & jnp.logical_not(inner))
        def _():
            arrived(3, 0)
            arrived(3, 1)

    def pick_rows(i):
        turn, k = place_of(i)
        base = (z * 2 + (x + turn) % 2) * per_dev
        named_rows, weights = routes_all[k], shares_all[k]
        line = lax.broadcasted_iota(jnp.int32, (8, tok_rows), 0)
        hits = jnp.zeros((8, tok_rows), F32)
        shares = []
        for e in range(per_dev):
            named = named_rows == base + e
            hit = jnp.max(jnp.where(named, F32(1), F32(0)), axis=0, keepdims=True)
            hits = hits + jnp.where(line == e, hit, F32(0))
            shares.append(jnp.sum(jnp.where(named, weights, F32(0)), axis=0, keepdims=True))
        counts[turn] += hits
        before = lax.broadcasted_iota(jnp.int32, (tok_rows, tok_rows), 0)
        after = lax.broadcasted_iota(jnp.int32, (tok_rows, tok_rows), 1)
        position = dot(hits.astype(BF16), one_hot(before < after))
        position = jnp.where(hits > 0, position, F32(-1)).astype(jnp.int32)
        slot_row = lax.broadcasted_iota(jnp.int32, (cap, tok_rows), 0)
        pick, mix = [], []
        for e in range(per_dev):
            chosen = slot_row == position[e : e + 1]
            pick.append(jnp.where(chosen, F32(1), F32(0)))
            mix.append(jnp.where(chosen, shares[e], F32(0)))
        pick = jnp.concatenate(pick, axis=0).astype(BF16)
        combine[i] = jnp.concatenate(mix, axis=0).T.astype(BF16)
        rows[...] = dot(pick, tok_all[k]).astype(BF16).reshape(per_dev, cap, features)

    def make_low(u):
        e = u % per_dev
        turn = u // per_dev // nz
        for h in range(2):
            weight = w1[turn, e, h * half : (h + 1) * half].reshape(half_width, dp * chunk)
            low = dot(rows[e, :, h * half_width : (h + 1) * half_width], weight).astype(BF16)
            for q in range(dp):
                low_out[u % ring, q, h] = low[:, q * chunk : (q + 1) * chunk]

    def send_low(u):
        for r in crossing:
            low_copy(u, r).start()
        low_local(u).start()

    def stage_a(u):
        @pl.when(u >= ring)
        def _():
            for r in crossing:
                low_copy(u - ring, r).wait_send()

        @pl.when(u % per_dev == 0)
        def _():
            meet(u // per_dev)
            pick_rows(u // per_dev)

        make_low(u)
        send_low(u)

    def stage_b(u):
        i, e = u // per_dev, u % per_dev
        turn = i // nz
        low_local(u).wait()
        for r in crossing:
            low_copy(u, r).wait_recv()

        @pl.when(u >= ring)
        def _():
            for r in crossing:
                down_copy(u - ring, r).wait_send()

        groups_of = []
        for lead in range(0, dp, 2):
            a, b, c_, d_ = [low_in[u, p, h] for p in (lead, lead + 1) for h in range(2)]
            a, c_ = swap_groups(a, c_, 64)
            b, d_ = swap_groups(b, d_, 64)
            a, b = swap_groups(a, b, 32)
            c_, d_ = swap_groups(c_, d_, 32)
            groups_of.append((a, b, c_, d_))
        high = [
            dot(jnp.concatenate([group[n] for group in groups_of], axis=1), w2[turn, e, n])
            for n in range(4)
        ]
        gate = jnp.concatenate(high[:2], axis=1)
        up = jnp.concatenate(high[2:], axis=1)
        activated = (gate / (1 + jnp.exp(-gate)) * up).astype(BF16)
        down = dot(activated, w3[turn, e]).astype(BF16)
        for p in range(dp):
            down_out[u % ring, p] = down[:, p * chunk : (p + 1) * chunk]
        for r in crossing:
            down_copy(u, r).start()
        down_local(u).start()

    def z_part(n, slot, to, h):
        return remote(z_out.at[n, h], z_in.at[slot, h], z_s.at[n, h], z_r.at[slot, h], at_z(to))

    def z_send(n, slot, to, h, value):
        z_out[n, h] = value.astype(BF16)
        z_part(n, slot, to, h).start()

    def z_wait(slot, h):
        z_part(0, slot, 1, h).wait_recv()

    def pass_far(h):
        z_wait(3, h)
        z_send(1, 4, 3, h, summed[2, h] + z_in[3, h].astype(F32))

    def pass_near(h):
        z_wait(4, h)
        z_send(0, 0, 1, h, summed[1, h] + z_in[4, h].astype(F32))

    def pass_across(h):
        z_wait(2, h)
        z_send(2, 5, 3, h, summed[3, h] + z_in[2, h].astype(F32))

    def stage_c(u):
        i, e = u // per_dev, u % per_dev
        turn, k = place_of(i)
        down_local(u).wait()
        for r in crossing:
            down_copy(u, r).wait_recv()
        pieces = [down_in[u, q] for q in range(dp)]
        low_a, high_a = swap_groups(pieces[0], pieces[1], 64)
        low_b, high_b = swap_groups(pieces[2], pieces[3], 64)
        for h, value in enumerate(((low_a, low_b), (high_a, high_b))):
            result = dot(jnp.concatenate(value, axis=1), w4[turn, e, h])
            made[h, e] = result.astype(BF16)

        @pl.when(e == per_dev - 1)
        def _():
            for h in range(2):
                part = dot(combine[i], made[h].reshape(per_dev * cap, half_width))

                @pl.when(turn == 0)
                def _():
                    summed[k, h] = part

                @pl.when((turn == 1) & ((k == 0) | inner))
                def _():
                    summed[k, h] += part

                for n in range(1, nz):

                    @pl.when((turn == 1) & (k == n) & jnp.logical_not(inner))
                    def _():
                        z_send(n - 1, n, 1, h, summed[n, h] + part)

    count_copy = remote(counts.at[1], counts_in, count_s.at[0], count_s.at[1], partner)

    for n in range(5):
        loads[n].wait()

    @pl.when(inner)
    def _():
        pl.semaphore_wait(barrier, len(peers) + 1)

    @pl.when(jnp.logical_not(inner))
    def _():
        pl.semaphore_wait(barrier, len(peers))

    for h in range(2):
        begin(gather(*sends[0], h))

        @pl.when(inner)
        def _():
            begin(gather(*sends[1], h))

    swap(0).start()
    swap(1).start()
    make_places()
    pick_rows(0)

    @pl.loop(0, per_dev)
    def _(u):
        spread_first(u, 0, gf, uf)
        make_low(u)
        send_low(u)

    for n in range(5, len(loads)):
        loads[n].wait()
    for e in range(per_dev):
        for c in range(rank_here):
            gs[e, c] = jnp.concatenate([gs_in[e, c], us_in[e, c]], axis=1)
        for c in range(pairs):
            df[e, c] = jnp.concatenate([df_in[e, c], df_in[e, c + pairs]], axis=1)
    for n in range(2, 5):
        swap(n).start()
    row3 = lax.broadcasted_iota(jnp.int32, (2 * block_count, hidden), 0)
    col3 = lax.broadcasted_iota(jnp.int32, (2 * block_count, hidden), 1)
    for c in range(rank_here):
        offset = (c // pairs) * block_count
        hit = (row3 >= offset) & (row3 < offset + block_count)
        place3[c] = one_hot(hit & (col3 == (row3 - offset) * rank_here + c))

    @pl.loop(0, per_dev)
    def _(u):
        spread_middle(u, 0, gs, df)
        stage_b(u)

        @pl.when(u == per_dev - 2)
        def _():
            pass_tokens(0)

    far_steps = nz * per_dev
    first_at, middle_at = far_steps - per_dev - 1, far_steps + 1
    last_at = far_steps + lag_c

    @pl.loop(per_dev, units + lag_c)
    def _(t):
        @pl.when((t >= first_at) & (t < first_at + per_dev))
        def _():
            @pl.when(t == first_at)
            def _():
                swap(0).wait_recv()
                swap(1).wait_recv()

            spread_first(t - first_at, 1, gf2, uf2)

        @pl.when(t == 2 * per_dev - 1)
        def _():
            pass_last(0)

        @pl.when(t < units)
        def _():
            stage_a(t)

        @pl.when((t >= middle_at) & (t < middle_at + per_dev))
        def _():
            @pl.when(t == middle_at)
            def _():
                swap(2).wait_recv()
                swap(3).wait_recv()

            spread_middle(t - middle_at, 1, gs2, df2)

        @pl.when((t >= lag_b + per_dev) & (t < units + lag_b))
        def _():
            stage_b(t - lag_b)

        @pl.when((t >= lag_c) & (t < lag_c + per_dev))
        def _():
            spread_last(t - lag_c, 0, ds)

        @pl.when((t >= last_at) & (t < last_at + per_dev))
        def _():
            @pl.when(t == last_at)
            def _():
                swap(4).wait_recv()

            spread_last(t - last_at, 1, ds2)

        @pl.when(t >= lag_c)
        def _():
            stage_c(t - lag_c)

        @pl.when(t == units)
        def _():
            count_copy.start()

        done_far = (steps - 2) * per_dev + lag_c - 1
        for h in range(2):

            @pl.when(inner & (t == done_far + h))
            def _():
                pass_far(h)

        @pl.when(inner & (t == done_far + per_dev))
        def _():
            pass_across(0)

        @pl.when(inner & (t == done_far + per_dev + 1))
        def _():
            pass_near(0)

    @pl.when(inner)
    def _():
        pass_near(1)
        pass_across(1)

    count_copy.wait()
    ones = jnp.ones((8, tok_rows), BF16)
    held_rows = lax.dot_general(
        ones, (counts[0] + counts_in[...]).astype(BF16),
        (((1,), (1,)), ((), ())), preferred_element_type=F32,
    )
    load[...] = held_rows[:1, :per_dev] * experts / (tok_rows * groups * top_k)

    for h in range(2):
        span = slice(h * half_width, (h + 1) * half_width)

        @pl.when(inner)
        def _():
            z_wait(1, h)
            z_wait(5, h)
            both = z_in[1, h].astype(F32) + z_in[5, h].astype(F32)
            out[:, span] = (summed[0, h] + both).astype(BF16)

        @pl.when(jnp.logical_not(inner))
        def _():
            z_wait(0, h)
            out[:, span] = (summed[0, h] + z_in[0, h].astype(F32)).astype(BF16)

    for h in range(2):
        for copy in gather(*sends[0], h):
            copy.wait_send()

        @pl.when(inner)
        def _():
            for link in (sends[1],) + relays:
                for copy in gather(*link, h):
                    copy.wait_send()

    for n in range(3):
        for h in range(2):
            z_part(n, 0, 1, h).wait_send()
    for n in range(len(held)):
        swap(n).wait_send()

    @pl.loop(units - ring, units)
    def _(u):
        for r in crossing:
            low_copy(u, r).wait_send()
            down_copy(u, r).wait_send()


def fused(
    tokens, routes, route_weight,
    gate_first, up_first, gate_second, up_second, down_first, down_second,
):
    tok_rows, features = tokens.shape
    top_k = routes.shape[1]
    groups = lax.axis_size("expert")
    dp = lax.axis_size("dp")
    per_dev, blocks, width, rank = gate_first.shape
    rank_here, block_count = gate_second.shape[1:3]
    experts = per_dev * groups
    cap = 2 * tok_rows * top_k // experts
    nz = groups // 2
    steps = 2 * nz
    units = steps * per_dev
    ring = 8
    half = blocks // 2
    chunk = 2 * rank_here * half
    hidden = rank_here * block_count
    slots = per_dev * cap
    pairs = rank_here // 2
    quad = pairs * block_count
    half_width = half * width
    first = (per_dev, blocks, rank, width)
    joined = (per_dev, rank_here, block_count, 2 * block_count)
    paired = (per_dev, pairs, block_count, 2 * block_count)
    second, last = gate_second.shape, down_second.shape
    vmem = pl.BlockSpec(memory_space=pltpu.VMEM)
    dma = pltpu.SemaphoreType.DMA
    out, load = pl.pallas_call(
        functools.partial(expert_kernel, (groups, dp, top_k, cap, rank_here, block_count)),
        out_shape=(
            jax.ShapeDtypeStruct((tok_rows, features), BF16),
            jax.ShapeDtypeStruct((1, per_dev), F32),
        ),
        in_specs=[pl.BlockSpec(memory_space=pl.ANY)] * 9,
        out_specs=(vmem, vmem),
        scratch_shapes=[
            pltpu.VMEM((nz, tok_rows, features), BF16),
            pltpu.VMEM((nz, top_k, tok_rows), jnp.int32),
            pltpu.VMEM((nz, top_k, tok_rows), F32),
            *[pltpu.VMEM(s, BF16) for s in (first, first, second, second, second, last)],
            *[pltpu.VMEM(s, BF16) for s in (joined, paired)],
            *[pltpu.VMEM(s, BF16) for s in (first, first, joined, paired, last)],
            pltpu.VMEM((2, per_dev, blocks, width, dp * chunk), BF16),
            pltpu.VMEM((2, per_dev, 4, quad, quad), BF16),
            pltpu.VMEM((2, per_dev, hidden, hidden), BF16),
            pltpu.VMEM((2, per_dev, 2, dp * chunk // 2, half_width), BF16),
            pltpu.VMEM((half, 2 * rank, dp * chunk), BF16),
            pltpu.VMEM((rank_here, 2 * block_count, hidden), BF16),
            pltpu.VMEM((per_dev, cap, features), BF16),
            pltpu.VMEM((ring, dp, 2, cap, chunk), BF16),
            pltpu.VMEM((units, dp, 2, cap, chunk), BF16),
            pltpu.VMEM((ring, dp, cap, chunk), BF16),
            pltpu.VMEM((units, dp, cap, chunk), BF16),
            pltpu.VMEM((steps, tok_rows, slots), BF16),
            pltpu.VMEM((2, per_dev, cap, half_width), BF16),
            pltpu.VMEM((nz, 2, tok_rows, half_width), F32),
            pltpu.VMEM((3, 2, tok_rows, half_width), BF16),
            pltpu.VMEM((6, 2, tok_rows, half_width), BF16),
            pltpu.VMEM((2, 8, tok_rows), F32),
            pltpu.VMEM((8, tok_rows), F32),
            dma((4, 5)), dma((4, nz)), dma((5,)), dma((5,)),
            dma((ring, dp)), dma((units, dp)), dma((ring, dp)), dma((units, dp)),
            dma((ring,)), dma((ring,)), dma((9,)), dma((2,)), dma((3, 2)), dma((6, 2)),
        ],
        compiler_params=pltpu.CompilerParams(
            collective_id=0, has_side_effects=True, vmem_limit_bytes=67043328
        ),
    )(
        tokens, routes.T, route_weight.T, gate_first.swapaxes(2, 3), up_first.swapaxes(2, 3),
        gate_second, up_second, down_first, down_second,
    )
    return (out, load.reshape(per_dev))


def chosen_plan(tokens, routes, route_weight, *weights):
    groups = lax.axis_size("expert")
    dp = lax.axis_size("dp")
    blocks, width = weights[0].shape[1:3]
    rank_here, block_count = weights[2].shape[1:3]
    tiled = (
        tokens.shape[0] % 128 == 0
        and 2 * rank_here * (blocks // 2) == 128
        and rank_here == 8
        and weights[0].shape[0] <= 8
        and blocks // 2 == 8
        and block_count == 2 * dp * 8
        and (blocks // 2 * width) % 128 == 0
    )
    powers = groups & (groups - 1) == 0 and dp & (dp - 1) == 0
    if groups <= 2 * routes.shape[1] and groups == 8 and dp == 4 and powers and tiled:
        return fused(tokens, routes, route_weight, *weights)
    return shards(tokens, routes, route_weight, *weights)


def solution(mesh):
    return jax.shard_map(
        chosen_plan,
        mesh=mesh,
        in_specs=(
            P("expert", "dp"),
            P("expert", None),
            P("expert", None),
            P("expert", "dp", None, None),
            P("expert", "dp", None, None),
            P("expert", "dp", None, None),
            P("expert", "dp", None, None),
            P("expert", "dp", None, None),
            P("expert", "dp", None, None),
        ),
        out_specs=(P("expert", "dp"), P("expert")),
        check_vma=False,
    )
```

```python
import functools

import jax
import jax.numpy as jnp
from jax import lax
from jax.experimental import pallas as pl
from jax.experimental.pallas import tpu as pltpu
from jax.sharding import PartitionSpec as P

F32 = jnp.float32
BF16 = jnp.bfloat16
MESH = pl.DeviceIdType.MESH
LAGS = (2, 4)


def shards(
    tokens,
    routes,
    route_weight,
    gate_first,
    up_first,
    gate_second,
    up_second,
    down_first,
    down_second,
):
    tok_rows, width_here = tokens.shape
    top_k = routes.shape[1]
    groups = lax.axis_size("expert")
    dp_count = lax.axis_size("dp")
    per_dev, blocks_here, block_width, rank_size = gate_first.shape
    rank_here = gate_second.shape[1]
    block_count = gate_second.shape[2]
    experts = per_dev * groups
    capacity = 2 * tok_rows * top_k // experts
    flat_routes = routes.reshape(-1)
    pair_count = flat_routes.shape[0]
    one_hot = (flat_routes[:, None] == jnp.arange(experts, dtype=jnp.int32)[None, :]).astype(
        jnp.int32
    )
    earlier = jnp.cumsum(one_hot, axis=0) - one_hot
    position = jnp.sum(earlier * one_hot, axis=1)
    counts = jnp.sum(one_hot, axis=0)
    slot_index = flat_routes * capacity + position
    pair_token = jnp.arange(pair_count, dtype=jnp.int32) // top_k
    slot_token = jnp.full((experts * capacity,), tok_rows, jnp.int32).at[slot_index].set(pair_token)
    outgoing = jnp.take(tokens, slot_token, axis=0, mode="fill", fill_value=0).reshape(
        groups, per_dev, capacity, width_here
    )
    gate_wide = gate_second.reshape(per_dev, rank_here, dp_count, blocks_here, block_count)
    up_wide = up_second.reshape(per_dev, rank_here, dp_count, blocks_here, block_count)
    down_wide = down_second.reshape(per_dev, blocks_here, dp_count, rank_here, block_width)
    received = lax.all_to_all(outgoing, "expert", split_axis=0, concat_axis=0, tiled=True)
    sources = received.shape[0]
    local = received.shape[1]
    slots = received.shape[2]
    split_rows = received.reshape(sources, local, slots, blocks_here, block_width)
    gate_low = jnp.einsum(
        "aesbf,ebfr->rbeas", split_rows, gate_first, preferred_element_type=jnp.float32
    )
    up_low = jnp.einsum(
        "aesbf,ebfr->rbeas", split_rows, up_first, preferred_element_type=jnp.float32
    )
    layout = (dp_count, rank_here, blocks_here, local, sources, slots)
    gate_mixed = lax.all_to_all(
        gate_low.astype(jnp.bfloat16).reshape(layout), "dp", split_axis=0, concat_axis=0, tiled=True
    )
    up_mixed = lax.all_to_all(
        up_low.astype(jnp.bfloat16).reshape(layout), "dp", split_axis=0, concat_axis=0, tiled=True
    )
    gate_high = jnp.einsum(
        "qcjeas,ecqjm->ecmas", gate_mixed, gate_wide, preferred_element_type=jnp.float32
    )
    up_high = jnp.einsum(
        "qcjeas,ecqjm->ecmas", up_mixed, up_wide, preferred_element_type=jnp.float32
    )
    activated = (jax.nn.silu(gate_high) * up_high).astype(jnp.bfloat16)
    down_low = jnp.einsum(
        "ecmas,ecmn->ecnas", activated, down_first, preferred_element_type=jnp.float32
    )
    down_split = down_low.astype(jnp.bfloat16).reshape(
        local, rank_here, dp_count, blocks_here, sources, slots
    )
    down_mixed = lax.all_to_all(down_split, "dp", split_axis=2, concat_axis=2, tiled=True)
    expert_out = jnp.einsum(
        "ecqjas,ejqcf->aesjf", down_mixed, down_wide, preferred_element_type=jnp.float32
    )
    result = expert_out.astype(jnp.bfloat16).reshape(sources, local, slots, width_here)
    totals = lax.psum(counts, "expert")
    own_counts = lax.dynamic_slice_in_dim(
        totals, lax.axis_index("expert") * per_dev, per_dev
    ).astype(jnp.float32)
    returned = lax.all_to_all(result, "expert", split_axis=0, concat_axis=0, tiled=True).reshape(
        experts * capacity, width_here
    )
    picked = jnp.take(returned, slot_index, axis=0).astype(jnp.float32)
    weighted = picked * route_weight.reshape(-1)[:, None]
    moe_output = jnp.sum(weighted.reshape(tok_rows, top_k, width_here), axis=1).astype(jnp.bfloat16)
    expert_load = own_counts * experts / (tok_rows * groups * top_k)
    return (moe_output, expert_load)


def xor(a, b, count):
    total, bit = 0, 1
    while bit < count:
        total = total + bit * ((a // bit + b // bit) % 2)
        bit *= 2
    return total


def dot(a, b):
    return jnp.dot(a, b, preferred_element_type=F32)


def one_hot(hit):
    return jnp.where(hit, F32(1), F32(0)).astype(BF16)


def swap_groups(a, b, size):
    lane = lax.broadcasted_iota(jnp.int32, a.shape, len(a.shape) - 1)
    even = (lane // size) % 2 == 0
    axis = len(a.shape) - 1
    first = jnp.where(even, a, pltpu.roll(b, size, axis))
    second = jnp.where(even, pltpu.roll(a, 128 - size, axis), b)
    return first, second


def expert_kernel(
    sizes,
    tok, routes, shares_in, gf_arg, uf_arg, gs_arg, us_arg, df_arg, ds_arg,
    out, load,
    tok_all, routes_all, shares_all, gf, uf, gs_in, us_in, df_in, ds,
    gs, df, gf2, uf2, gs2, df2, ds2,
    w1, w2, w3, w4, place1, place3, rows,
    low_out, low_in, down_out, down_in,
    combine, made, summed, z_out, z_in, counts, counts_in,
    gather_s, gather_r, weight_s, weight_r, low_s, low_r, down_s, down_r,
    local_low, local_down, load_s, count_s, z_s, z_r,
):
    groups, dp, top_k, cap, rank_here, block_count = sizes
    per_dev, blocks, rank, width = gf.shape
    tok_rows, features = tok.shape
    experts = per_dev * groups
    half = blocks // 2
    half_width = half * width
    chunk = 2 * rank_here * half
    hidden = rank_here * block_count
    pairs = rank_here // 2
    quad = pairs * block_count
    nz = groups // 2
    steps = 2 * nz
    units = steps * per_dev
    ring = low_out.shape[0]
    lag_b, lag_c = LAGS
    d = lax.axis_index("dp")
    g = lax.axis_index("expert")
    z, x = g // 2, g % 2
    partner = (d, z * 2 + (1 - x))
    inner = (z >= 1) & (z < nz - 1)

    def at_dp(r):
        return (xor(d, r, dp), g)

    def at_z(k):
        return (d, xor(z, k, nz) * 2 + x)

    def remote(src, dst, send, recv, to):
        return pltpu.make_async_remote_copy(
            src_ref=src, dst_ref=dst, send_sem=send, recv_sem=recv,
            device_id=to, device_id_type=MESH,
        )

    barrier = pltpu.get_barrier_semaphore()
    peers = [at_dp(r) for r in range(1, dp)] + [partner, at_z(1)]

    def greet(peer):
        pl.semaphore_signal(barrier, inc=1, device_id=peer, device_id_type=MESH)

    for peer in peers:
        greet(peer)

    @pl.when(inner)
    def _():
        greet(at_z(3))

    inputs = (
        (gf_arg, gf), (uf_arg, uf), (routes, routes_all.at[0]), (shares_in, shares_all.at[0]),
        (tok, tok_all.at[0]), (gs_arg, gs_in), (us_arg, us_in), (df_arg, df_in), (ds_arg, ds),
    )
    loads = [
        pltpu.make_async_copy(src, dst, load_s.at[n]) for n, (src, dst) in enumerate(inputs)
    ]
    for copy in loads:
        copy.start()

    part_rows = tok_rows // 2

    def gather(link, source, to, slot, h):
        rows_of = pl.ds(h * part_rows, part_rows)
        pairs_of = [(tok_all.at[source, rows_of], tok_all.at[slot, rows_of])]
        if h == 0:
            pairs_of += [(ref.at[source], ref.at[slot]) for ref in (routes_all, shares_all)]
        return [
            remote(src, dst, gather_s.at[n + 3 * h, link], gather_r.at[n + 3 * h, slot], at_z(to))
            for n, (src, dst) in enumerate(pairs_of)
        ]

    def begin(copies):
        for copy in copies:
            copy.start()

    sends = ((0, 0, 1, 1), (1, 0, 3, 3))
    relays = ((2, 1, 3, 2), (3, 3, 1, 2), (4, 2, 1, 3))

    def arrived(slot, h):
        for copy in gather(0, 0, 1, slot, h):
            copy.wait_recv()

    held = (gf, uf, gs, df, ds)
    swapped = (gf2, uf2, gs2, df2, ds2)

    def swap(n):
        return remote(held[n], swapped[n], weight_s.at[n], weight_r.at[n], partner)

    counts[...] = jnp.zeros_like(counts)
    def make_places():
        row1 = lax.broadcasted_iota(jnp.int32, (2 * rank, dp * chunk), 0)
        col1 = lax.broadcasted_iota(jnp.int32, (2 * rank, dp * chunk), 1)
        side1, rest1 = row1 // rank, row1 % rank
        base1 = (rest1 // rank_here) * chunk + side1 * (chunk // 2) + (rest1 % rank_here) * half
        for j in range(half):
            place1[j] = one_hot(col1 == base1 + j)

    def spread_first(e, turn, gate, up):
        for b in range(blocks):
            both = jnp.concatenate([gate[e, b], up[e, b]], axis=0)
            w1[turn, e, b] = lax.dot_general(
                both, place1[b % half], (((0,), (0,)), ((), ())), preferred_element_type=F32
            ).astype(BF16)

    def spread_middle(e, turn, second, third):
        lane = lax.broadcasted_iota(jnp.int32, (block_count, 128), 1)
        low_half = lane < block_count
        nothing = jnp.zeros((block_count // half, half, 128), F32)
        for part in range(rank_here // pairs):
            tiles = ([], [])
            for c in range(pairs):
                value = second[e, part * pairs + c].astype(F32)
                turned = pltpu.roll(value, block_count, 1)
                for side in range(2):
                    if c % 2 == 0:
                        kept = jnp.where(low_half, value if side == 0 else turned, F32(0))
                    else:
                        kept = jnp.where(low_half, F32(0), turned if side == 0 else value)
                    kept = kept.reshape(block_count // half, half, 128)
                    spots = [nothing] * (quad // 128)
                    spots[c // 2] = kept
                    tiles[side].append(jnp.concatenate(spots, axis=2))
            for side in range(2):
                tile = jnp.stack(tiles[side], axis=1).reshape(quad, quad)
                w2[turn, e, side * (rank_here // pairs) + part] = tile.astype(BF16)
        for c in range(rank_here):
            value = dot(third[e, c % pairs], place3[c])
            w3[turn, e, c * block_count : (c + 1) * block_count] = value.astype(BF16)

    def spread_last(e, turn, fourth):
        lane = lax.broadcasted_iota(jnp.int32, (rank, 128), 1)
        nothing = jnp.zeros((dp, rank_here, 128), F32)
        for h in range(2):
            stripes = []
            for n in range(half):
                value = fourth[e, h * half + n].astype(F32)
                value = jnp.concatenate(
                    [value, jnp.zeros((rank, 128 - width), F32)], axis=1
                )
                spot, shift = (n * width) // 128, (n * width) % 128
                spots = [nothing] * (half_width // 128)
                if shift == 0:
                    spots[spot] = value.reshape(dp, rank_here, 128)
                else:
                    turned = pltpu.roll(value, shift, 1)
                    spots[spot] = jnp.where(lane >= shift, turned, F32(0)).reshape(
                        dp, rank_here, 128
                    )
                    if shift + width > 128:
                        spots[spot + 1] = jnp.where(lane < shift, turned, F32(0)).reshape(
                            dp, rank_here, 128
                        )
                stripes.append(jnp.concatenate(spots, axis=2))
            tile = jnp.stack(stripes, axis=1).reshape(dp * chunk // 2, half_width)
            w4[turn, e, h] = tile.astype(BF16)

    def place_of(i):
        turn = i // nz
        return turn, (i % nz) * (1 - turn) + (nz - 1 - i % nz) * turn

    def low_copy(u, r):
        return remote(
            low_out.at[u % ring, xor(d, r, dp)], low_in.at[u, d],
            low_s.at[u % ring, r], low_r.at[u, r], at_dp(r),
        )

    def down_copy(u, r):
        return remote(
            down_out.at[u % ring, xor(d, r, dp)], down_in.at[u, d],
            down_s.at[u % ring, r], down_r.at[u, r], at_dp(r),
        )

    def low_local(u):
        return pltpu.make_async_copy(
            low_out.at[u % ring, d], low_in.at[u, d], local_low.at[u % ring]
        )

    def down_local(u):
        return pltpu.make_async_copy(
            down_out.at[u % ring, d], down_in.at[u, d], local_down.at[u % ring]
        )

    crossing = list(range(dp - 1, 0, -1))

    def pass_tokens(h):
        arrived(1, h)

        @pl.when(inner)
        def _():
            begin(gather(*relays[0], h))
            arrived(3, h)
            begin(gather(*relays[1], h))

    def pass_last(h):
        arrived(2, h)

        @pl.when(inner)
        def _():
            begin(gather(*relays[2], h))

    def meet(i):
        @pl.when(i == 1)
        def _():
            pass_tokens(1)

        @pl.when(i == 2)
        def _():
            pass_last(1)

        @pl.when((i == 3) & jnp.logical_not(inner))
        def _():
            arrived(3, 0)
            arrived(3, 1)

    def pick_rows(i):
        turn, k = place_of(i)
        base = (z * 2 + (x + turn) % 2) * per_dev
        named_rows, weights = routes_all[k], shares_all[k]
        line = lax.broadcasted_iota(jnp.int32, (8, tok_rows), 0)
        hits = jnp.zeros((8, tok_rows), F32)
        shares = []
        for e in range(per_dev):
            named = named_rows == base + e
            hit = jnp.max(jnp.where(named, F32(1), F32(0)), axis=0, keepdims=True)
            hits = hits + jnp.where(line == e, hit, F32(0))
            shares.append(jnp.sum(jnp.where(named, weights, F32(0)), axis=0, keepdims=True))
        counts[turn] += hits
        before = lax.broadcasted_iota(jnp.int32, (tok_rows, tok_rows), 0)
        after = lax.broadcasted_iota(jnp.int32, (tok_rows, tok_rows), 1)
        position = dot(hits.astype(BF16), one_hot(before < after))
        position = jnp.where(hits > 0, position, F32(-1)).astype(jnp.int32)
        slot_row = lax.broadcasted_iota(jnp.int32, (cap, tok_rows), 0)
        pick, mix = [], []
        for e in range(per_dev):
            chosen = slot_row == position[e : e + 1]
            pick.append(jnp.where(chosen, F32(1), F32(0)))
            mix.append(jnp.where(chosen, shares[e], F32(0)))
        pick = jnp.concatenate(pick, axis=0).astype(BF16)
        combine[i] = jnp.concatenate(mix, axis=0).T.astype(BF16)
        rows[...] = dot(pick, tok_all[k]).astype(BF16).reshape(per_dev, cap, features)

    def make_low(u):
        e = u % per_dev
        turn = u // per_dev // nz
        for h in range(2):
            weight = w1[turn, e, h * half : (h + 1) * half].reshape(half_width, dp * chunk)
            low = dot(rows[e, :, h * half_width : (h + 1) * half_width], weight).astype(BF16)
            for q in range(dp):
                low_out[u % ring, q, h] = low[:, q * chunk : (q + 1) * chunk]

    def send_low(u):
        for r in crossing:
            low_copy(u, r).start()
        low_local(u).start()

    def stage_a(u):
        @pl.when(u >= ring)
        def _():
            for r in crossing:
                low_copy(u - ring, r).wait_send()

        @pl.when(u % per_dev == 0)
        def _():
            meet(u // per_dev)
            pick_rows(u // per_dev)

        make_low(u)
        send_low(u)

    def stage_b(u):
        i, e = u // per_dev, u % per_dev
        turn = i // nz
        low_local(u).wait()
        for r in crossing:
            low_copy(u, r).wait_recv()

        @pl.when(u >= ring)
        def _():
            for r in crossing:
                down_copy(u - ring, r).wait_send()

        groups_of = []
        for lead in range(0, dp, 2):
            a, b, c_, d_ = [low_in[u, p, h] for p in (lead, lead + 1) for h in range(2)]
            a, c_ = swap_groups(a, c_, 64)
            b, d_ = swap_groups(b, d_, 64)
            a, b = swap_groups(a, b, 32)
            c_, d_ = swap_groups(c_, d_, 32)
            groups_of.append((a, b, c_, d_))
        high = [
            dot(jnp.concatenate([group[n] for group in groups_of], axis=1), w2[turn, e, n])
            for n in range(4)
        ]
        gate = jnp.concatenate(high[:2], axis=1)
        up = jnp.concatenate(high[2:], axis=1)
        activated = (gate / (1 + jnp.exp(-gate)) * up).astype(BF16)
        down = dot(activated, w3[turn, e]).astype(BF16)
        for p in range(dp):
            down_out[u % ring, p] = down[:, p * chunk : (p + 1) * chunk]
        for r in crossing:
            down_copy(u, r).start()
        down_local(u).start()

    def z_part(n, slot, to, h):
        return remote(z_out.at[n, h], z_in.at[slot, h], z_s.at[n, h], z_r.at[slot, h], at_z(to))

    def z_send(n, slot, to, h, value):
        z_out[n, h] = value.astype(BF16)
        z_part(n, slot, to, h).start()

    def z_wait(slot, h):
        z_part(0, slot, 1, h).wait_recv()

    def pass_far(h):
        z_wait(3, h)
        z_send(1, 4, 3, h, summed[2, h] + z_in[3, h].astype(F32))

    def pass_near(h):
        z_wait(4, h)
        z_send(0, 0, 1, h, summed[1, h] + z_in[4, h].astype(F32))

    def pass_across(h):
        z_wait(2, h)
        z_send(2, 5, 3, h, summed[3, h] + z_in[2, h].astype(F32))

    def stage_c(u):
        i, e = u // per_dev, u % per_dev
        turn, k = place_of(i)
        down_local(u).wait()
        for r in crossing:
            down_copy(u, r).wait_recv()
        pieces = [down_in[u, q] for q in range(dp)]
        low_a, high_a = swap_groups(pieces[0], pieces[1], 64)
        low_b, high_b = swap_groups(pieces[2], pieces[3], 64)
        for h, value in enumerate(((low_a, low_b), (high_a, high_b))):
            result = dot(jnp.concatenate(value, axis=1), w4[turn, e, h])
            made[h, e] = result.astype(BF16)

        @pl.when(e == per_dev - 1)
        def _():
            for h in range(2):
                part = dot(combine[i], made[h].reshape(per_dev * cap, half_width))

                @pl.when(turn == 0)
                def _():
                    summed[k, h] = part

                @pl.when((turn == 1) & ((k == 0) | inner))
                def _():
                    summed[k, h] += part

                for n in range(1, nz):

                    @pl.when((turn == 1) & (k == n) & jnp.logical_not(inner))
                    def _():
                        z_send(n - 1, n, 1, h, summed[n, h] + part)

    count_copy = remote(counts.at[1], counts_in, count_s.at[0], count_s.at[1], partner)

    for n in range(5):
        loads[n].wait()

    @pl.when(inner)
    def _():
        pl.semaphore_wait(barrier, len(peers) + 1)

    @pl.when(jnp.logical_not(inner))
    def _():
        pl.semaphore_wait(barrier, len(peers))

    for h in range(2):
        begin(gather(*sends[0], h))

        @pl.when(inner)
        def _():
            begin(gather(*sends[1], h))

    swap(0).start()
    swap(1).start()
    make_places()
    pick_rows(0)

    @pl.loop(0, per_dev)
    def _(u):
        spread_first(u, 0, gf, uf)
        make_low(u)
        send_low(u)

    for n in range(5, len(loads)):
        loads[n].wait()
    for e in range(per_dev):
        for c in range(rank_here):
            gs[e, c] = jnp.concatenate([gs_in[e, c], us_in[e, c]], axis=1)
        for c in range(pairs):
            df[e, c] = jnp.concatenate([df_in[e, c], df_in[e, c + pairs]], axis=1)
    for n in range(2, 5):
        swap(n).start()
    row3 = lax.broadcasted_iota(jnp.int32, (2 * block_count, hidden), 0)
    col3 = lax.broadcasted_iota(jnp.int32, (2 * block_count, hidden), 1)
    for c in range(rank_here):
        offset = (c // pairs) * block_count
        hit = (row3 >= offset) & (row3 < offset + block_count)
        place3[c] = one_hot(hit & (col3 == (row3 - offset) * rank_here + c))

    @pl.loop(0, per_dev)
    def _(u):
        spread_middle(u, 0, gs, df)
        stage_b(u)

        @pl.when(u == per_dev - 2)
        def _():
            pass_tokens(0)

    far_steps = nz * per_dev
    first_at, middle_at = far_steps - per_dev - 1, far_steps + 1
    last_at = far_steps + lag_c

    @pl.loop(per_dev, units + lag_c)
    def _(t):
        @pl.when((t >= first_at) & (t < first_at + per_dev))
        def _():
            @pl.when(t == first_at)
            def _():
                swap(0).wait_recv()
                swap(1).wait_recv()

            spread_first(t - first_at, 1, gf2, uf2)

        @pl.when(t == 2 * per_dev - 1)
        def _():
            pass_last(0)

        @pl.when(t < units)
        def _():
            stage_a(t)

        @pl.when((t >= middle_at) & (t < middle_at + per_dev))
        def _():
            @pl.when(t == middle_at)
            def _():
                swap(2).wait_recv()
                swap(3).wait_recv()

            spread_middle(t - middle_at, 1, gs2, df2)

        @pl.when((t >= lag_b + per_dev) & (t < units + lag_b))
        def _():
            stage_b(t - lag_b)

        @pl.when((t >= lag_c) & (t < lag_c + per_dev))
        def _():
            spread_last(t - lag_c, 0, ds)

        @pl.when((t >= last_at) & (t < last_at + per_dev))
        def _():
            @pl.when(t == last_at)
            def _():
                swap(4).wait_recv()

            spread_last(t - last_at, 1, ds2)

        @pl.when(t >= lag_c)
        def _():
            stage_c(t - lag_c)

        @pl.when(t == units)
        def _():
            count_copy.start()

        done_far = (steps - 2) * per_dev + lag_c - 1
        @pl.when(inner & (t == done_far + 0))
        def _():
            pass_far(0)

        @pl.when(inner & (t == done_far + 1))
        def _():
            pass_far(1)

        @pl.when(inner & (t == done_far + 5))
        def _():
            pass_across(0)

        @pl.when(inner & (t == done_far + 7))
        def _():
            pass_across(1)

        @pl.when(inner & (t == done_far + 4))
        def _():
            pass_near(0)

        @pl.when(inner & (t == done_far + 5))
        def _():
            pass_near(1)

    count_copy.wait()
    ones = jnp.ones((8, tok_rows), BF16)
    held_rows = lax.dot_general(
        ones, (counts[0] + counts_in[...]).astype(BF16),
        (((1,), (1,)), ((), ())), preferred_element_type=F32,
    )
    load[...] = held_rows[:1, :per_dev] * experts / (tok_rows * groups * top_k)

    for h in range(2):
        span = slice(h * half_width, (h + 1) * half_width)

        @pl.when(inner)
        def _():
            z_wait(1, h)
            z_wait(5, h)
            both = z_in[1, h].astype(F32) + z_in[5, h].astype(F32)
            out[:, span] = (summed[0, h] + both).astype(BF16)

        @pl.when(jnp.logical_not(inner))
        def _():
            z_wait(0, h)
            out[:, span] = (summed[0, h] + z_in[0, h].astype(F32)).astype(BF16)

    for h in range(2):
        for copy in gather(*sends[0], h):
            copy.wait_send()

        @pl.when(inner)
        def _():
            for link in (sends[1],) + relays:
                for copy in gather(*link, h):
                    copy.wait_send()

    for n in range(3):
        for h in range(2):
            z_part(n, 0, 1, h).wait_send()
    for n in range(len(held)):
        swap(n).wait_send()

    @pl.loop(units - ring, units)
    def _(u):
        for r in crossing:
            low_copy(u, r).wait_send()
            down_copy(u, r).wait_send()


def fused(
    tokens, routes, route_weight,
    gate_first, up_first, gate_second, up_second, down_first, down_second,
):
    tok_rows, features = tokens.shape
    top_k = routes.shape[1]
    groups = lax.axis_size("expert")
    dp = lax.axis_size("dp")
    per_dev, blocks, width, rank = gate_first.shape
    rank_here, block_count = gate_second.shape[1:3]
    experts = per_dev * groups
    cap = 2 * tok_rows * top_k // experts
    nz = groups // 2
    steps = 2 * nz
    units = steps * per_dev
    ring = 8
    half = blocks // 2
    chunk = 2 * rank_here * half
    hidden = rank_here * block_count
    slots = per_dev * cap
    pairs = rank_here // 2
    quad = pairs * block_count
    half_width = half * width
    first = (per_dev, blocks, rank, width)
    joined = (per_dev, rank_here, block_count, 2 * block_count)
    paired = (per_dev, pairs, block_count, 2 * block_count)
    second, last = gate_second.shape, down_second.shape
    vmem = pl.BlockSpec(memory_space=pltpu.VMEM)
    dma = pltpu.SemaphoreType.DMA
    out, load = pl.pallas_call(
        functools.partial(expert_kernel, (groups, dp, top_k, cap, rank_here, block_count)),
        out_shape=(
            jax.ShapeDtypeStruct((tok_rows, features), BF16),
            jax.ShapeDtypeStruct((1, per_dev), F32),
        ),
        in_specs=[pl.BlockSpec(memory_space=pl.ANY)] * 9,
        out_specs=(vmem, vmem),
        scratch_shapes=[
            pltpu.VMEM((nz, tok_rows, features), BF16),
            pltpu.VMEM((nz, top_k, tok_rows), jnp.int32),
            pltpu.VMEM((nz, top_k, tok_rows), F32),
            *[pltpu.VMEM(s, BF16) for s in (first, first, second, second, second, last)],
            *[pltpu.VMEM(s, BF16) for s in (joined, paired)],
            *[pltpu.VMEM(s, BF16) for s in (first, first, joined, paired, last)],
            pltpu.VMEM((2, per_dev, blocks, width, dp * chunk), BF16),
            pltpu.VMEM((2, per_dev, 4, quad, quad), BF16),
            pltpu.VMEM((2, per_dev, hidden, hidden), BF16),
            pltpu.VMEM((2, per_dev, 2, dp * chunk // 2, half_width), BF16),
            pltpu.VMEM((half, 2 * rank, dp * chunk), BF16),
            pltpu.VMEM((rank_here, 2 * block_count, hidden), BF16),
            pltpu.VMEM((per_dev, cap, features), BF16),
            pltpu.VMEM((ring, dp, 2, cap, chunk), BF16),
            pltpu.VMEM((units, dp, 2, cap, chunk), BF16),
            pltpu.VMEM((ring, dp, cap, chunk), BF16),
            pltpu.VMEM((units, dp, cap, chunk), BF16),
            pltpu.VMEM((steps, tok_rows, slots), BF16),
            pltpu.VMEM((2, per_dev, cap, half_width), BF16),
            pltpu.VMEM((nz, 2, tok_rows, half_width), F32),
            pltpu.VMEM((3, 2, tok_rows, half_width), BF16),
            pltpu.VMEM((6, 2, tok_rows, half_width), BF16),
            pltpu.VMEM((2, 8, tok_rows), F32),
            pltpu.VMEM((8, tok_rows), F32),
            dma((4, 5)), dma((4, nz)), dma((5,)), dma((5,)),
            dma((ring, dp)), dma((units, dp)), dma((ring, dp)), dma((units, dp)),
            dma((ring,)), dma((ring,)), dma((9,)), dma((2,)), dma((3, 2)), dma((6, 2)),
        ],
        compiler_params=pltpu.CompilerParams(
            collective_id=0, has_side_effects=True, vmem_limit_bytes=67043328
        ),
    )(
        tokens, routes.T, route_weight.T, gate_first.swapaxes(2, 3), up_first.swapaxes(2, 3),
        gate_second, up_second, down_first, down_second,
    )
    return (out, load.reshape(per_dev))


def chosen_plan(tokens, routes, route_weight, *weights):
    groups = lax.axis_size("expert")
    dp = lax.axis_size("dp")
    blocks, width = weights[0].shape[1:3]
    rank_here, block_count = weights[2].shape[1:3]
    tiled = (
        tokens.shape[0] % 128 == 0
        and 2 * rank_here * (blocks // 2) == 128
        and rank_here == 8
        and weights[0].shape[0] <= 8
        and blocks // 2 == 8
        and block_count == 2 * dp * 8
        and (blocks // 2 * width) % 128 == 0
    )
    powers = groups & (groups - 1) == 0 and dp & (dp - 1) == 0
    if groups <= 2 * routes.shape[1] and groups == 8 and dp == 4 and powers and tiled:
        return fused(tokens, routes, route_weight, *weights)
    return shards(tokens, routes, route_weight, *weights)


def solution(mesh):
    return jax.shard_map(
        chosen_plan,
        mesh=mesh,
        in_specs=(
            P("expert", "dp"),
            P("expert", None),
            P("expert", None),
            P("expert", "dp", None, None),
            P("expert", "dp", None, None),
            P("expert", "dp", None, None),
            P("expert", "dp", None, None),
            P("expert", "dp", None, None),
            P("expert", "dp", None, None),
        ),
        out_specs=(P("expert", "dp"), P("expert")),
        check_vma=False,
    )
```

```python
import functools

import jax
import jax.numpy as jnp
from jax import lax
from jax.experimental import pallas as pl
from jax.experimental.pallas import tpu as pltpu
from jax.sharding import PartitionSpec as P

F32 = jnp.float32
BF16 = jnp.bfloat16
MESH = pl.DeviceIdType.MESH
LAGS = (2, 4)


def shards(
    tokens,
    routes,
    route_weight,
    gate_first,
    up_first,
    gate_second,
    up_second,
    down_first,
    down_second,
):
    tok_rows, width_here = tokens.shape
    top_k = routes.shape[1]
    groups = lax.axis_size("expert")
    dp_count = lax.axis_size("dp")
    per_dev, blocks_here, block_width, rank_size = gate_first.shape
    rank_here = gate_second.shape[1]
    block_count = gate_second.shape[2]
    experts = per_dev * groups
    capacity = 2 * tok_rows * top_k // experts
    flat_routes = routes.reshape(-1)
    pair_count = flat_routes.shape[0]
    one_hot = (flat_routes[:, None] == jnp.arange(experts, dtype=jnp.int32)[None, :]).astype(
        jnp.int32
    )
    earlier = jnp.cumsum(one_hot, axis=0) - one_hot
    position = jnp.sum(earlier * one_hot, axis=1)
    counts = jnp.sum(one_hot, axis=0)
    slot_index = flat_routes * capacity + position
    pair_token = jnp.arange(pair_count, dtype=jnp.int32) // top_k
    slot_token = jnp.full((experts * capacity,), tok_rows, jnp.int32).at[slot_index].set(pair_token)
    outgoing = jnp.take(tokens, slot_token, axis=0, mode="fill", fill_value=0).reshape(
        groups, per_dev, capacity, width_here
    )
    gate_wide = gate_second.reshape(per_dev, rank_here, dp_count, blocks_here, block_count)
    up_wide = up_second.reshape(per_dev, rank_here, dp_count, blocks_here, block_count)
    down_wide = down_second.reshape(per_dev, blocks_here, dp_count, rank_here, block_width)
    received = lax.all_to_all(outgoing, "expert", split_axis=0, concat_axis=0, tiled=True)
    sources = received.shape[0]
    local = received.shape[1]
    slots = received.shape[2]
    split_rows = received.reshape(sources, local, slots, blocks_here, block_width)
    gate_low = jnp.einsum(
        "aesbf,ebfr->rbeas", split_rows, gate_first, preferred_element_type=jnp.float32
    )
    up_low = jnp.einsum(
        "aesbf,ebfr->rbeas", split_rows, up_first, preferred_element_type=jnp.float32
    )
    layout = (dp_count, rank_here, blocks_here, local, sources, slots)
    gate_mixed = lax.all_to_all(
        gate_low.astype(jnp.bfloat16).reshape(layout), "dp", split_axis=0, concat_axis=0, tiled=True
    )
    up_mixed = lax.all_to_all(
        up_low.astype(jnp.bfloat16).reshape(layout), "dp", split_axis=0, concat_axis=0, tiled=True
    )
    gate_high = jnp.einsum(
        "qcjeas,ecqjm->ecmas", gate_mixed, gate_wide, preferred_element_type=jnp.float32
    )
    up_high = jnp.einsum(
        "qcjeas,ecqjm->ecmas", up_mixed, up_wide, preferred_element_type=jnp.float32
    )
    activated = (jax.nn.silu(gate_high) * up_high).astype(jnp.bfloat16)
    down_low = jnp.einsum(
        "ecmas,ecmn->ecnas", activated, down_first, preferred_element_type=jnp.float32
    )
    down_split = down_low.astype(jnp.bfloat16).reshape(
        local, rank_here, dp_count, blocks_here, sources, slots
    )
    down_mixed = lax.all_to_all(down_split, "dp", split_axis=2, concat_axis=2, tiled=True)
    expert_out = jnp.einsum(
        "ecqjas,ejqcf->aesjf", down_mixed, down_wide, preferred_element_type=jnp.float32
    )
    result = expert_out.astype(jnp.bfloat16).reshape(sources, local, slots, width_here)
    totals = lax.psum(counts, "expert")
    own_counts = lax.dynamic_slice_in_dim(
        totals, lax.axis_index("expert") * per_dev, per_dev
    ).astype(jnp.float32)
    returned = lax.all_to_all(result, "expert", split_axis=0, concat_axis=0, tiled=True).reshape(
        experts * capacity, width_here
    )
    picked = jnp.take(returned, slot_index, axis=0).astype(jnp.float32)
    weighted = picked * route_weight.reshape(-1)[:, None]
    moe_output = jnp.sum(weighted.reshape(tok_rows, top_k, width_here), axis=1).astype(jnp.bfloat16)
    expert_load = own_counts * experts / (tok_rows * groups * top_k)
    return (moe_output, expert_load)


def xor(a, b, count):
    total, bit = 0, 1
    while bit < count:
        total = total + bit * ((a // bit + b // bit) % 2)
        bit *= 2
    return total


def dot(a, b):
    return jnp.dot(a, b, preferred_element_type=F32)


def one_hot(hit):
    return jnp.where(hit, F32(1), F32(0)).astype(BF16)


def swap_groups(a, b, size):
    lane = lax.broadcasted_iota(jnp.int32, a.shape, len(a.shape) - 1)
    even = (lane // size) % 2 == 0
    axis = len(a.shape) - 1
    first = jnp.where(even, a, pltpu.roll(b, size, axis))
    second = jnp.where(even, pltpu.roll(a, 128 - size, axis), b)
    return first, second


def expert_kernel(
    sizes,
    tok, routes, shares_in, gf_arg, uf_arg, gs_arg, us_arg, df_arg, ds_arg,
    out, load,
    tok_all, routes_all, shares_all, gf, uf, gs_in, us_in, df_in, ds,
    gs, df, gf2, uf2, gs2, df2, ds2,
    w1, w2, w3, w4, place1, place3, rows,
    low_out, low_in, down_out, down_in,
    combine, made, summed, z_out, z_in, counts, counts_in,
    gather_s, gather_r, weight_s, weight_r, low_s, low_r, down_s, down_r,
    local_low, local_down, load_s, count_s, z_s, z_r,
):
    groups, dp, top_k, cap, rank_here, block_count = sizes
    per_dev, blocks, rank, width = gf.shape
    tok_rows, features = tok.shape
    experts = per_dev * groups
    half = blocks // 2
    half_width = half * width
    chunk = 2 * rank_here * half
    hidden = rank_here * block_count
    pairs = rank_here // 2
    quad = pairs * block_count
    nz = groups // 2
    steps = 2 * nz
    units = steps * per_dev
    ring = low_out.shape[0]
    lag_b, lag_c = LAGS
    d = lax.axis_index("dp")
    g = lax.axis_index("expert")
    z, x = g // 2, g % 2
    partner = (d, z * 2 + (1 - x))
    inner = (z >= 1) & (z < nz - 1)

    def at_dp(r):
        return (xor(d, r, dp), g)

    def at_z(k):
        return (d, xor(z, k, nz) * 2 + x)

    def remote(src, dst, send, recv, to):
        return pltpu.make_async_remote_copy(
            src_ref=src, dst_ref=dst, send_sem=send, recv_sem=recv,
            device_id=to, device_id_type=MESH,
        )

    barrier = pltpu.get_barrier_semaphore()
    peers = [at_dp(r) for r in range(1, dp)] + [partner, at_z(1)]

    def greet(peer):
        pl.semaphore_signal(barrier, inc=1, device_id=peer, device_id_type=MESH)

    for peer in peers:
        greet(peer)

    @pl.when(inner)
    def _():
        greet(at_z(3))

    inputs = (
        (gf_arg, gf), (uf_arg, uf), (routes, routes_all.at[0]), (shares_in, shares_all.at[0]),
        (tok, tok_all.at[0]), (gs_arg, gs_in), (us_arg, us_in), (df_arg, df_in), (ds_arg, ds),
    )
    loads = [
        pltpu.make_async_copy(src, dst, load_s.at[n]) for n, (src, dst) in enumerate(inputs)
    ]
    for copy in loads:
        copy.start()

    part_rows = tok_rows // 2

    def gather(link, source, to, slot, h):
        rows_of = pl.ds(h * part_rows, part_rows)
        pairs_of = [(tok_all.at[source, rows_of], tok_all.at[slot, rows_of])]
        if h == 0:
            pairs_of += [(ref.at[source], ref.at[slot]) for ref in (routes_all, shares_all)]
        return [
            remote(src, dst, gather_s.at[n + 3 * h, link], gather_r.at[n + 3 * h, slot], at_z(to))
            for n, (src, dst) in enumerate(pairs_of)
        ]

    def begin(copies):
        for copy in copies:
            copy.start()

    sends = ((0, 0, 1, 1), (1, 0, 3, 3))
    relays = ((2, 1, 3, 2), (3, 3, 1, 2), (4, 2, 1, 3))

    def arrived(slot, h):
        for copy in gather(0, 0, 1, slot, h):
            copy.wait_recv()

    held = (gf, uf, gs, df, ds)
    swapped = (gf2, uf2, gs2, df2, ds2)

    def swap(n):
        return remote(held[n], swapped[n], weight_s.at[n], weight_r.at[n], partner)

    counts[...] = jnp.zeros_like(counts)
    def make_places():
        row1 = lax.broadcasted_iota(jnp.int32, (2 * rank, dp * chunk), 0)
        col1 = lax.broadcasted_iota(jnp.int32, (2 * rank, dp * chunk), 1)
        side1, rest1 = row1 // rank, row1 % rank
        base1 = (rest1 // rank_here) * chunk + side1 * (chunk // 2) + (rest1 % rank_here) * half
        for j in range(half):
            place1[j] = one_hot(col1 == base1 + j)

    def spread_first(e, turn, gate, up):
        for b in range(blocks):
            both = jnp.concatenate([gate[e, b], up[e, b]], axis=0)
            w1[turn, e, b] = lax.dot_general(
                both, place1[b % half], (((0,), (0,)), ((), ())), preferred_element_type=F32
            ).astype(BF16)

    def spread_middle(e, turn, second, third):
        lane = lax.broadcasted_iota(jnp.int32, (block_count, 128), 1)
        low_half = lane < block_count
        nothing = jnp.zeros((block_count // half, half, 128), F32)
        for part in range(rank_here // pairs):
            tiles = ([], [])
            for c in range(pairs):
                value = second[e, part * pairs + c].astype(F32)
                turned = pltpu.roll(value, block_count, 1)
                for side in range(2):
                    if c % 2 == 0:
                        kept = jnp.where(low_half, value if side == 0 else turned, F32(0))
                    else:
                        kept = jnp.where(low_half, F32(0), turned if side == 0 else value)
                    kept = kept.reshape(block_count // half, half, 128)
                    spots = [nothing] * (quad // 128)
                    spots[c // 2] = kept
                    tiles[side].append(jnp.concatenate(spots, axis=2))
            for side in range(2):
                tile = jnp.stack(tiles[side], axis=1).reshape(quad, quad)
                w2[turn, e, side * (rank_here // pairs) + part] = tile.astype(BF16)
        for c in range(rank_here):
            value = dot(third[e, c % pairs], place3[c])
            w3[turn, e, c * block_count : (c + 1) * block_count] = value.astype(BF16)

    def spread_last(e, turn, fourth):
        lane = lax.broadcasted_iota(jnp.int32, (rank, 128), 1)
        nothing = jnp.zeros((dp, rank_here, 128), F32)
        for h in range(2):
            stripes = []
            for n in range(half):
                value = fourth[e, h * half + n].astype(F32)
                value = jnp.concatenate(
                    [value, jnp.zeros((rank, 128 - width), F32)], axis=1
                )
                spot, shift = (n * width) // 128, (n * width) % 128
                spots = [nothing] * (half_width // 128)
                if shift == 0:
                    spots[spot] = value.reshape(dp, rank_here, 128)
                else:
                    turned = pltpu.roll(value, shift, 1)
                    spots[spot] = jnp.where(lane >= shift, turned, F32(0)).reshape(
                        dp, rank_here, 128
                    )
                    if shift + width > 128:
                        spots[spot + 1] = jnp.where(lane < shift, turned, F32(0)).reshape(
                            dp, rank_here, 128
                        )
                stripes.append(jnp.concatenate(spots, axis=2))
            tile = jnp.stack(stripes, axis=1).reshape(dp * chunk // 2, half_width)
            w4[turn, e, h] = tile.astype(BF16)

    def place_of(i):
        turn = i // nz
        return turn, (i % nz) * (1 - turn) + (nz - 1 - i % nz) * turn

    def low_copy(u, r):
        return remote(
            low_out.at[u % ring, xor(d, r, dp)], low_in.at[u, d],
            low_s.at[u % ring, r], low_r.at[u, r], at_dp(r),
        )

    def down_copy(u, r):
        return remote(
            down_out.at[u % ring, xor(d, r, dp)], down_in.at[u, d],
            down_s.at[u % ring, r], down_r.at[u, r], at_dp(r),
        )

    def low_local(u):
        return pltpu.make_async_copy(
            low_out.at[u % ring, d], low_in.at[u, d], local_low.at[u % ring]
        )

    def down_local(u):
        return pltpu.make_async_copy(
            down_out.at[u % ring, d], down_in.at[u, d], local_down.at[u % ring]
        )

    crossing = list(range(dp - 1, 0, -1))

    def pass_tokens(h):
        arrived(1, h)

        @pl.when(inner)
        def _():
            begin(gather(*relays[0], h))
            arrived(3, h)
            begin(gather(*relays[1], h))

    def pass_last(h):
        arrived(2, h)

        @pl.when(inner)
        def _():
            begin(gather(*relays[2], h))

    def meet(i):
        @pl.when(i == 1)
        def _():
            pass_tokens(1)

        @pl.when(i == 2)
        def _():
            pass_last(1)

        @pl.when((i == 3) & jnp.logical_not(inner))
        def _():
            arrived(3, 0)
            arrived(3, 1)

    def pick_rows(i):
        turn, k = place_of(i)
        base = (z * 2 + (x + turn) % 2) * per_dev
        named_rows, weights = routes_all[k], shares_all[k]
        line = lax.broadcasted_iota(jnp.int32, (8, tok_rows), 0)
        hits = jnp.zeros((8, tok_rows), F32)
        shares = []
        for e in range(per_dev):
            named = named_rows == base + e
            hit = jnp.max(jnp.where(named, F32(1), F32(0)), axis=0, keepdims=True)
            hits = hits + jnp.where(line == e, hit, F32(0))
            shares.append(jnp.sum(jnp.where(named, weights, F32(0)), axis=0, keepdims=True))
        counts[turn] += hits
        before = lax.broadcasted_iota(jnp.int32, (tok_rows, tok_rows), 0)
        after = lax.broadcasted_iota(jnp.int32, (tok_rows, tok_rows), 1)
        position = dot(hits.astype(BF16), one_hot(before < after))
        position = jnp.where(hits > 0, position, F32(-1)).astype(jnp.int32)
        slot_row = lax.broadcasted_iota(jnp.int32, (cap, tok_rows), 0)
        pick, mix = [], []
        for e in range(per_dev):
            chosen = slot_row == position[e : e + 1]
            pick.append(jnp.where(chosen, F32(1), F32(0)))
            mix.append(jnp.where(chosen, shares[e], F32(0)))
        pick = jnp.concatenate(pick, axis=0).astype(BF16)
        combine[i] = jnp.concatenate(mix, axis=0).T.astype(BF16)
        rows[...] = dot(pick, tok_all[k]).astype(BF16).reshape(per_dev, cap, features)

    def make_low(u):
        e = u % per_dev
        turn = u // per_dev // nz
        for h in range(2):
            weight = w1[turn, e, h * half : (h + 1) * half].reshape(half_width, dp * chunk)
            low = dot(rows[e, :, h * half_width : (h + 1) * half_width], weight).astype(BF16)
            for q in range(dp):
                low_out[u % ring, q, h] = low[:, q * chunk : (q + 1) * chunk]

    def send_low(u):
        for r in crossing:
            low_copy(u, r).start()
        low_local(u).start()

    def stage_a(u):
        @pl.when(u >= ring)
        def _():
            for r in crossing:
                low_copy(u - ring, r).wait_send()

        @pl.when(u % per_dev == 0)
        def _():
            meet(u // per_dev)
            pick_rows(u // per_dev)

        make_low(u)
        send_low(u)

    def stage_b(u):
        i, e = u // per_dev, u % per_dev
        turn = i // nz
        low_local(u).wait()
        for r in crossing:
            low_copy(u, r).wait_recv()

        @pl.when(u >= ring)
        def _():
            for r in crossing:
                down_copy(u - ring, r).wait_send()

        groups_of = []
        for lead in range(0, dp, 2):
            a, b, c_, d_ = [low_in[u, p, h] for p in (lead, lead + 1) for h in range(2)]
            a, c_ = swap_groups(a, c_, 64)
            b, d_ = swap_groups(b, d_, 64)
            a, b = swap_groups(a, b, 32)
            c_, d_ = swap_groups(c_, d_, 32)
            groups_of.append((a, b, c_, d_))
        high = [
            dot(jnp.concatenate([group[n] for group in groups_of], axis=1), w2[turn, e, n])
            for n in range(4)
        ]
        gate = jnp.concatenate(high[:2], axis=1)
        up = jnp.concatenate(high[2:], axis=1)
        activated = (gate / (1 + jnp.exp(-gate)) * up).astype(BF16)
        down = dot(activated, w3[turn, e]).astype(BF16)
        for p in range(dp):
            down_out[u % ring, p] = down[:, p * chunk : (p + 1) * chunk]
        for r in crossing:
            down_copy(u, r).start()
        down_local(u).start()

    def z_part(n, slot, to, h):
        return remote(z_out.at[n, h], z_in.at[slot, h], z_s.at[n, h], z_r.at[slot, h], at_z(to))

    def z_send(n, slot, to, h, value):
        z_out[n, h] = value.astype(BF16)
        z_part(n, slot, to, h).start()

    def z_wait(slot, h):
        z_part(0, slot, 1, h).wait_recv()

    def pass_far(h):
        z_wait(3, h)
        z_send(1, 4, 3, h, summed[2, h] + z_in[3, h].astype(F32))

    def pass_near(h):
        z_wait(4, h)
        z_send(0, 0, 1, h, summed[1, h] + z_in[4, h].astype(F32))

    def pass_across(h):
        z_wait(2, h)
        z_send(2, 5, 3, h, summed[3, h] + z_in[2, h].astype(F32))

    def stage_c(u):
        i, e = u // per_dev, u % per_dev
        turn, k = place_of(i)
        down_local(u).wait()
        for r in crossing:
            down_copy(u, r).wait_recv()
        pieces = [down_in[u, q] for q in range(dp)]
        low_a, high_a = swap_groups(pieces[0], pieces[1], 64)
        low_b, high_b = swap_groups(pieces[2], pieces[3], 64)
        for h, value in enumerate(((low_a, low_b), (high_a, high_b))):
            result = dot(jnp.concatenate(value, axis=1), w4[turn, e, h])
            made[h, e] = result.astype(BF16)

        @pl.when(e == per_dev - 1)
        def _():
            for h in range(2):
                part = dot(combine[i], made[h].reshape(per_dev * cap, half_width))

                @pl.when(turn == 0)
                def _():
                    summed[k, h] = part

                @pl.when((turn == 1) & ((k == 0) | inner))
                def _():
                    summed[k, h] += part

                for n in range(1, nz):

                    @pl.when((turn == 1) & (k == n) & jnp.logical_not(inner))
                    def _():
                        z_send(n - 1, n, 1, h, summed[n, h] + part)

    count_copy = remote(counts.at[1], counts_in, count_s.at[0], count_s.at[1], partner)

    for n in range(5):
        loads[n].wait()

    @pl.when(inner)
    def _():
        pl.semaphore_wait(barrier, len(peers) + 1)

    @pl.when(jnp.logical_not(inner))
    def _():
        pl.semaphore_wait(barrier, len(peers))

    for h in range(2):
        begin(gather(*sends[0], h))

        @pl.when(inner)
        def _():
            begin(gather(*sends[1], h))

    swap(0).start()
    swap(1).start()
    make_places()
    pick_rows(0)

    @pl.loop(0, per_dev)
    def _(u):
        spread_first(u, 0, gf, uf)
        make_low(u)
        send_low(u)

    for n in range(5, len(loads)):
        loads[n].wait()
    for e in range(per_dev):
        for c in range(rank_here):
            gs[e, c] = jnp.concatenate([gs_in[e, c], us_in[e, c]], axis=1)
        for c in range(pairs):
            df[e, c] = jnp.concatenate([df_in[e, c], df_in[e, c + pairs]], axis=1)
    for n in range(2, 5):
        swap(n).start()
    row3 = lax.broadcasted_iota(jnp.int32, (2 * block_count, hidden), 0)
    col3 = lax.broadcasted_iota(jnp.int32, (2 * block_count, hidden), 1)
    for c in range(rank_here):
        offset = (c // pairs) * block_count
        hit = (row3 >= offset) & (row3 < offset + block_count)
        place3[c] = one_hot(hit & (col3 == (row3 - offset) * rank_here + c))

    @pl.loop(0, per_dev)
    def _(u):
        spread_middle(u, 0, gs, df)
        stage_b(u)

        @pl.when(u == per_dev - 2)
        def _():
            pass_tokens(0)

    far_steps = nz * per_dev
    first_at, middle_at = far_steps - per_dev - 1, far_steps + 1
    last_at = far_steps + lag_c

    @pl.loop(per_dev, units + lag_c)
    def _(t):
        @pl.when((t >= first_at) & (t < first_at + per_dev))
        def _():
            @pl.when(t == first_at)
            def _():
                swap(0).wait_recv()
                swap(1).wait_recv()

            spread_first(t - first_at, 1, gf2, uf2)

        @pl.when(t == 2 * per_dev - 1)
        def _():
            pass_last(0)

        @pl.when(t < units)
        def _():
            stage_a(t)

        @pl.when((t >= middle_at) & (t < middle_at + per_dev))
        def _():
            @pl.when(t == middle_at)
            def _():
                swap(2).wait_recv()
                swap(3).wait_recv()

            spread_middle(t - middle_at, 1, gs2, df2)

        @pl.when((t >= lag_b + per_dev) & (t < units + lag_b))
        def _():
            stage_b(t - lag_b)

        @pl.when((t >= lag_c) & (t < lag_c + per_dev))
        def _():
            spread_last(t - lag_c, 0, ds)

        @pl.when((t >= last_at) & (t < last_at + per_dev))
        def _():
            @pl.when(t == last_at)
            def _():
                swap(4).wait_recv()

            spread_last(t - last_at, 1, ds2)

        @pl.when(t >= lag_c)
        def _():
            stage_c(t - lag_c)

        @pl.when(t == units)
        def _():
            count_copy.start()

        done_far = (steps - 2) * per_dev + lag_c - 1
        @pl.when(inner & (t == done_far + 0))
        def _():
            pass_far(0)

        @pl.when(inner & (t == done_far + 1))
        def _():
            pass_far(1)

        @pl.when(inner & (t == done_far + 6))
        def _():
            pass_across(0)

        @pl.when(inner & (t == done_far + 7))
        def _():
            pass_across(1)

        @pl.when(inner & (t == done_far + 4))
        def _():
            pass_near(0)

        @pl.when(inner & (t == done_far + 5))
        def _():
            pass_near(1)

    count_copy.wait()
    ones = jnp.ones((8, tok_rows), BF16)
    held_rows = lax.dot_general(
        ones, (counts[0] + counts_in[...]).astype(BF16),
        (((1,), (1,)), ((), ())), preferred_element_type=F32,
    )
    load[...] = held_rows[:1, :per_dev] * experts / (tok_rows * groups * top_k)

    for h in range(2):
        span = slice(h * half_width, (h + 1) * half_width)

        @pl.when(inner)
        def _():
            z_wait(1, h)
            z_wait(5, h)
            both = z_in[1, h].astype(F32) + z_in[5, h].astype(F32)
            out[:, span] = (summed[0, h] + both).astype(BF16)

        @pl.when(jnp.logical_not(inner))
        def _():
            z_wait(0, h)
            out[:, span] = (summed[0, h] + z_in[0, h].astype(F32)).astype(BF16)

    for h in range(2):
        for copy in gather(*sends[0], h):
            copy.wait_send()

        @pl.when(inner)
        def _():
            for link in (sends[1],) + relays:
                for copy in gather(*link, h):
                    copy.wait_send()

    for n in range(3):
        for h in range(2):
            z_part(n, 0, 1, h).wait_send()
    for n in range(len(held)):
        swap(n).wait_send()

    @pl.loop(units - ring, units)
    def _(u):
        for r in crossing:
            low_copy(u, r).wait_send()
            down_copy(u, r).wait_send()


def fused(
    tokens, routes, route_weight,
    gate_first, up_first, gate_second, up_second, down_first, down_second,
):
    tok_rows, features = tokens.shape
    top_k = routes.shape[1]
    groups = lax.axis_size("expert")
    dp = lax.axis_size("dp")
    per_dev, blocks, width, rank = gate_first.shape
    rank_here, block_count = gate_second.shape[1:3]
    experts = per_dev * groups
    cap = 2 * tok_rows * top_k // experts
    nz = groups // 2
    steps = 2 * nz
    units = steps * per_dev
    ring = 8
    half = blocks // 2
    chunk = 2 * rank_here * half
    hidden = rank_here * block_count
    slots = per_dev * cap
    pairs = rank_here // 2
    quad = pairs * block_count
    half_width = half * width
    first = (per_dev, blocks, rank, width)
    joined = (per_dev, rank_here, block_count, 2 * block_count)
    paired = (per_dev, pairs, block_count, 2 * block_count)
    second, last = gate_second.shape, down_second.shape
    vmem = pl.BlockSpec(memory_space=pltpu.VMEM)
    dma = pltpu.SemaphoreType.DMA
    out, load = pl.pallas_call(
        functools.partial(expert_kernel, (groups, dp, top_k, cap, rank_here, block_count)),
        out_shape=(
            jax.ShapeDtypeStruct((tok_rows, features), BF16),
            jax.ShapeDtypeStruct((1, per_dev), F32),
        ),
        in_specs=[pl.BlockSpec(memory_space=pl.ANY)] * 9,
        out_specs=(vmem, vmem),
        scratch_shapes=[
            pltpu.VMEM((nz, tok_rows, features), BF16),
            pltpu.VMEM((nz, top_k, tok_rows), jnp.int32),
            pltpu.VMEM((nz, top_k, tok_rows), F32),
            *[pltpu.VMEM(s, BF16) for s in (first, first, second, second, second, last)],
            *[pltpu.VMEM(s, BF16) for s in (joined, paired)],
            *[pltpu.VMEM(s, BF16) for s in (first, first, joined, paired, last)],
            pltpu.VMEM((2, per_dev, blocks, width, dp * chunk), BF16),
            pltpu.VMEM((2, per_dev, 4, quad, quad), BF16),
            pltpu.VMEM((2, per_dev, hidden, hidden), BF16),
            pltpu.VMEM((2, per_dev, 2, dp * chunk // 2, half_width), BF16),
            pltpu.VMEM((half, 2 * rank, dp * chunk), BF16),
            pltpu.VMEM((rank_here, 2 * block_count, hidden), BF16),
            pltpu.VMEM((per_dev, cap, features), BF16),
            pltpu.VMEM((ring, dp, 2, cap, chunk), BF16),
            pltpu.VMEM((units, dp, 2, cap, chunk), BF16),
            pltpu.VMEM((ring, dp, cap, chunk), BF16),
            pltpu.VMEM((units, dp, cap, chunk), BF16),
            pltpu.VMEM((steps, tok_rows, slots), BF16),
            pltpu.VMEM((2, per_dev, cap, half_width), BF16),
            pltpu.VMEM((nz, 2, tok_rows, half_width), F32),
            pltpu.VMEM((3, 2, tok_rows, half_width), BF16),
            pltpu.VMEM((6, 2, tok_rows, half_width), BF16),
            pltpu.VMEM((2, 8, tok_rows), F32),
            pltpu.VMEM((8, tok_rows), F32),
            dma((4, 5)), dma((4, nz)), dma((5,)), dma((5,)),
            dma((ring, dp)), dma((units, dp)), dma((ring, dp)), dma((units, dp)),
            dma((ring,)), dma((ring,)), dma((9,)), dma((2,)), dma((3, 2)), dma((6, 2)),
        ],
        compiler_params=pltpu.CompilerParams(
            collective_id=0, has_side_effects=True, vmem_limit_bytes=67043328
        ),
    )(
        tokens, routes.T, route_weight.T, gate_first.swapaxes(2, 3), up_first.swapaxes(2, 3),
        gate_second, up_second, down_first, down_second,
    )
    return (out, load.reshape(per_dev))


def chosen_plan(tokens, routes, route_weight, *weights):
    groups = lax.axis_size("expert")
    dp = lax.axis_size("dp")
    blocks, width = weights[0].shape[1:3]
    rank_here, block_count = weights[2].shape[1:3]
    tiled = (
        tokens.shape[0] % 128 == 0
        and 2 * rank_here * (blocks // 2) == 128
        and rank_here == 8
        and weights[0].shape[0] <= 8
        and blocks // 2 == 8
        and block_count == 2 * dp * 8
        and (blocks // 2 * width) % 128 == 0
    )
    powers = groups & (groups - 1) == 0 and dp & (dp - 1) == 0
    if groups <= 2 * routes.shape[1] and groups == 8 and dp == 4 and powers and tiled:
        return fused(tokens, routes, route_weight, *weights)
    return shards(tokens, routes, route_weight, *weights)


def solution(mesh):
    return jax.shard_map(
        chosen_plan,
        mesh=mesh,
        in_specs=(
            P("expert", "dp"),
            P("expert", None),
            P("expert", None),
            P("expert", "dp", None, None),
            P("expert", "dp", None, None),
            P("expert", "dp", None, None),
            P("expert", "dp", None, None),
            P("expert", "dp", None, None),
            P("expert", "dp", None, None),
        ),
        out_specs=(P("expert", "dp"), P("expert")),
        check_vma=False,
    )
```
